256 devices in a mesh: seq: 4 (over x_lo, core), ctx: 64 (over x_hi, z, y).
Axes of the slice: x: 4 (x_hi: 2, x_lo: 2; x = x_hi * 2 + x_lo), y: 4, z: 8, core: 2. Of those that a mesh axis runs over, the one named last changes fastest.
Arguments:
- grad_out: bfloat16 [4, 8192, 4096], P('seq', 'ctx'), may hold values from -6 to 6
- inputs: bfloat16 [4, 8192, 4096], P('seq', 'ctx'), may hold values from -6 to 6
- residues: float32 [16, 256], replicated, may hold values from -4 to 4
- rates: float32 [16, 256], replicated, may hold values from 1.2207031e-05 to 0.0625
Outputs:
- grad_in: float32 [4, 8192, 4096], P('seq', 'ctx')
- grad_residues: float32 [16, 256], replicated
The draws below stay inside these ranges and needn't reach their ends.
All inputs are finite; a program needn't handle non-finite values.
Results may differ from the reference program's by a relative error of at most 0.0003.
Values sent between devices are 32-bit elements; how exact they have to be, the bound alone decides.
No kernel may reach another device: no remote copies, remote signals or barrier semaphores. Data moves between devices by JAX's collectives and lax.ppermute only.
A program may use at most 128 MiB of HBM per device.

```python
import jax
import jax.numpy as jnp
from jax import lax

D = 4096
G = 256
CG = 16
MODES = 16
TOKENS = 8192
SEQS = 4


def draw_rates(key, part):
    base_key = jax.random.fold_in(key, 11)
    coin_key, slow_key, fast_key = jax.random.split(base_key, 3)
    slow_unit = jax.random.uniform(slow_key, (MODES, G), jnp.float32)
    fast_unit = jax.random.uniform(fast_key, (MODES, G), jnp.float32)
    slow_low = jnp.log(0.25 / TOKENS)
    middle = jnp.log(2.3 / TOKENS)
    fast_high = jnp.log(0.0625)
    slow_rate = jnp.exp(slow_low + slow_unit * (middle - slow_low))
    fast_rate = jnp.exp(middle + fast_unit * (fast_high - middle))
    coin = jax.random.randint(coin_key, (MODES, G), 0, 2, dtype=jnp.int32)
    return jnp.where(coin == 1, slow_rate, fast_rate).astype(jnp.float32)


def block_scale(key, shape, pieces, low, high):
    level, own = 1.0, jax.random.fold_in(key, 6)
    for dim, parts in pieces:
        heights = jnp.exp(jax.random.uniform(jax.random.fold_in(own, dim), (parts,), jnp.float32, low / len(pieces), high / len(pieces)))
        level = level * jnp.repeat(heights, shape[dim] // parts).reshape([-1 if axis == dim else 1 for axis in range(len(shape))])
    return level


def noise(key, dims, width, limit, pieces=(), held_as=jnp.bfloat16):
    array = width * jax.random.normal(key, dims, jnp.float32)
    if pieces:
        array = array * block_scale(key, dims, pieces, -0.22, 0.18)
    return jnp.clip(array, -limit, limit).astype(held_as)


def setup_inputs(seed: int = 0) -> dict:
    arg_keys = jax.random.split(jax.random.key(seed), 5)
    grad_out = noise(arg_keys[0], (SEQS, TOKENS, D), 1.0, 6.0, ((0, 4), (1, 64)))
    inputs = noise(arg_keys[1], (SEQS, TOKENS, D), 1.0, 6.0, ((0, 4), (1, 64)))
    residues = noise(arg_keys[2], (MODES, G), 1.0, 4.0, (), jnp.float32)
    rates = draw_rates(jax.random.fold_in(arg_keys[4], 71), 0)
    return dict(grad_out=grad_out, inputs=inputs, residues=residues, rates=rates)


def reference(grad_out, inputs, residues, rates):
    fft_len = 2 * TOKENS
    chan_block = CG * min(G, 16)
    group_block = chan_block // CG
    lag_axis = jnp.arange(TOKENS, dtype=jnp.float32)
    amplitude = residues * jnp.sqrt(-jnp.expm1(-2.0 * rates) / MODES)
    kernel = jnp.zeros((TOKENS, G), jnp.float32)
    for which in range(MODES):
        kernel = kernel + amplitude[which][None, :] * jnp.exp(-rates[which][None, :] * lag_axis[:, None])
    spectrum = jnp.fft.rfft(kernel, n=fft_len, axis=0)

    def one_block(position):
        first_chan = (position * chan_block).astype(jnp.int32)
        first_group = (position * group_block).astype(jnp.int32)
        grad_block = lax.dynamic_slice_in_dim(grad_out, first_chan, chan_block, 2).astype(jnp.float32)
        input_block = lax.dynamic_slice_in_dim(inputs, first_chan, chan_block, 2).astype(jnp.float32)
        grad_freq = jnp.fft.rfft(grad_block, n=fft_len, axis=1)
        input_freq = jnp.fft.rfft(input_block, n=fft_len, axis=1)
        group_freq = lax.dynamic_slice_in_dim(spectrum, first_group, group_block, 1)
        chan_freq = jnp.repeat(group_freq, CG, axis=1)
        grad_rows = jnp.fft.irfft(jnp.conj(chan_freq)[None] * grad_freq, n=fft_len, axis=1)[:, :TOKENS]
        cross = (jnp.conj(input_freq) * grad_freq).reshape(SEQS, -1, group_block, CG).sum(axis=(0, 3))
        lagged = jnp.fft.irfft(cross, n=fft_len, axis=0)[:TOKENS]
        return (grad_rows, lagged)
    grad_blocks, lag_blocks = lax.map(one_block, jnp.arange(D // chan_block, dtype=jnp.int32))
    grad_in = jnp.moveaxis(grad_blocks, 0, 2).reshape(SEQS, TOKENS, D)
    lag_all = jnp.moveaxis(lag_blocks, 0, 1).reshape(TOKENS, G)
    sums = jnp.stack([lax.optimization_barrier(jnp.sum(jnp.exp(-rates[which][None, :] * lag_axis[:, None]) * lag_all, axis=0)) for which in range(MODES)])
    factor = jnp.sqrt(-jnp.expm1(-2.0 * rates) / float(SEQS * TOKENS * CG))
    return (grad_in, sums * factor)
```

```python
import functools

import jax
import jax.numpy as jnp
from jax import lax
from jax.experimental import pallas as pl
from jax.experimental.pallas import tpu as pltpu
from jax.sharding import Mesh
from jax.sharding import PartitionSpec as P

CTX = ("ctx_0", "ctx_1", "ctx_2")
LANES = 128
CG = 16
GT = LANES // CG
SUB = 32
F32 = jnp.float32
BF16 = jnp.bfloat16
HIGHEST = lax.Precision.HIGHEST


def iota(shape, dim):
    return lax.broadcasted_iota(jnp.int32, shape, dim)


def split(value):
    high = value.astype(BF16)
    return high, (value - high.astype(F32)).astype(BF16)


def dot(a, b, dims=((1,), (0,))):
    return lax.dot_general(a, b, (dims, ((), ())), preferred_element_type=F32)


def group_columns(table, first):
    groups = table.shape[1]
    turned = pltpu.roll(table, (groups - first) % groups, 1)
    return [jnp.broadcast_to(turned[:, g : g + 1], (table.shape[0], LANES)) for g in range(GT)]


def own_group(full, rows):
    group_of = iota((rows, LANES), 1) // CG
    kept = full[:rows]
    for g in range(1, GT):
        kept = jnp.where(group_of == g, full[g * rows : (g + 1) * rows], kept)
    return kept


def summary_kernel(rates_ref, grad_ref, in_ref, out_ref):
    rows = grad_ref.shape[0]
    modes = rates_ref.shape[0]
    half = modes // 2
    tiles = grad_ref.shape[1] // LANES
    all_tiles = out_ref.shape[0] // (2 * 17)
    pos = iota((modes, LANES), 1).astype(F32)
    lane_group = iota((GT, LANES), 1) // CG
    own = lane_group == iota((GT, LANES), 0)
    lane = iota((GT, LANES), 1)
    cell = iota((half, LANES), 1)
    cell_row = iota((half, LANES), 0)

    def one_tile(k, carry):
        tile = pl.program_id(0) * tiles + k
        at = pl.ds(pl.multiple_of(k * LANES, LANES), LANES)
        grad = grad_ref[:, at]
        inp = in_ref[:, at]
        columns = group_columns(rates_ref[...], tile * GT)
        decays = [jnp.exp(-r * pos) for r in columns]
        decay = jnp.concatenate(decays, 0)
        tails = jnp.concatenate([jnp.exp(-r * (rows - pos)) for r in columns], 0)
        left = jnp.concatenate(split(decay), 1)
        summary = own_group(dot(left, jnp.concatenate([grad, grad], 0)), modes)
        left = jnp.concatenate(split(tails), 1)
        tail = own_group(dot(left, jnp.concatenate([inp, inp], 0)), modes)

        wide = inp.astype(F32)
        lefts = []
        rights = []
        for i in range(rows // SUB):
            piece = wide[i * SUB : (i + 1) * SUB]
            spread = jnp.broadcast_to(piece[:, None, :], (SUB, GT, LANES))
            spread = jnp.where(own[None], spread, 0.0)
            lefts.append(spread.reshape(SUB * GT, LANES).astype(BF16))
            window = grad[i * SUB :]
            if i:
                window = jnp.concatenate([window, jnp.zeros((i * SUB, LANES), BF16)], 0)
            rights.append(window)
        pairs = dot(jnp.concatenate(lefts, 1), jnp.concatenate(rights, 1), ((1,), (1,)))
        lagged = pairs[:GT]
        for j in range(1, SUB):
            part = jnp.where(lane >= j, pairs[j * GT : (j + 1) * GT], 0.0)
            lagged = lagged + pltpu.roll(part, LANES - j, 1)
        sums = [jnp.zeros((half, LANES), F32) for _ in range(2)]
        for g in range(GT):
            weighted = decays[g] * lagged[g : g + 1]
            total = jnp.sum(weighted, axis=1, keepdims=True)
            place = cell == cell_row + g * CG
            for a in range(2):
                sums[a] = jnp.where(place, total[a * half : (a + 1) * half], sums[a])
        for a in range(2):
            base = (a * all_tiles + tile) * 17
            out_ref[pl.ds(base, 8), :] = summary[a * half : (a + 1) * half]
            out_ref[pl.ds(base + 8, 8), :] = tail[a * half : (a + 1) * half]
            out_ref[pl.ds(base + 16, 1), :] = jnp.sum(sums[a], axis=0, keepdims=True)
        return carry

    lax.fori_loop(0, tiles, one_tile, 0, unroll=2)


def local_kernel(rates_ref, amp_ref, rate_row_ref, amp_row_ref, grad_ref, out_ref, high_ref, low_ref):
    rows = grad_ref.shape[0]
    modes = rates_ref.shape[0]
    tiles = grad_ref.shape[1] // LANES
    pos = iota((modes, LANES), 1).astype(F32)
    ahead = iota((SUB, LANES), 1) >= iota((SUB, LANES), 0)
    to_end = (rows - iota((rows, LANES), 0)).astype(F32)

    def one_tile(k, carry):
        tile = pl.program_id(0) * tiles + k
        at = pl.ds(pl.multiple_of(k * LANES, LANES), LANES)
        grad = grad_ref[:, at]
        columns = group_columns(rates_ref[...], tile * GT)
        amps = group_columns(amp_ref[...], tile * GT)
        highs = []
        lows = []
        for r, a in zip(columns, amps):
            kernel = jnp.sum(a * jnp.exp(-r * pos), axis=0, keepdims=True)
            high = kernel.astype(BF16).astype(F32)
            for part, into in ((high, highs), (kernel - high, lows)):
                turned = pltpu.roll(
                    jnp.broadcast_to(part, (SUB, LANES)), 0, 1, stride=1, stride_axis=0
                )
                into.append(jnp.where(ahead, turned, 0.0).astype(BF16))
        left = jnp.concatenate([jnp.concatenate(highs, 0), jnp.concatenate(lows, 0)], 1)
        for i in range(rows // SUB):
            window = grad[i * SUB :]
            if i:
                window = jnp.concatenate([window, jnp.zeros((i * SUB, LANES), BF16)], 0)
            full = dot(left, jnp.concatenate([window, window], 0))
            out_ref[i * SUB : (i + 1) * SUB, at] = own_group(full, SUB)
        weight = amp_row_ref[:, at] * jnp.exp(-rate_row_ref[:, at] * to_end)
        high, low = split(weight)
        high_ref[:, at] = high
        low_ref[:, at] = low
        return carry

    lax.fori_loop(0, tiles, one_tile, 0, unroll=2)


def scan_kernel(decay_ref, in_ref, out_ref):
    shards = in_ref.shape[0] // 17
    decay = decay_ref[...]
    state = jnp.zeros((8, LANES), F32)
    total = jnp.zeros((8, LANES), F32)
    row = jnp.zeros((1, LANES), F32)
    for j in reversed(range(shards)):
        out_ref[9 * j : 9 * j + 8, :] = state
        total = total + in_ref[17 * j + 8 : 17 * j + 16, :] * state
        row = row + in_ref[17 * j + 16 : 17 * j + 17, :]
        state = in_ref[17 * j : 17 * j + 8, :] + decay * state
    same = iota((LANES, LANES), 0) // CG == iota((LANES, LANES), 1) // CG
    summed = lax.dot_general(
        total,
        same.astype(F32),
        (((1,), (0,)), ((), ())),
        precision=HIGHEST,
        preferred_element_type=F32,
    )
    place = iota((8, LANES), 1) % CG == iota((8, LANES), 0)
    row = row + jnp.sum(jnp.where(place, summed, 0.0), axis=0, keepdims=True)
    for j in range(shards):
        out_ref[9 * j + 8 : 9 * j + 9, :] = row


def carry_kernel(state_ref, local_ref, high_ref, low_ref, out_ref):
    tiles = out_ref.shape[1] // LANES
    all_tiles = state_ref.shape[0] // (2 * 9)
    lane_group = iota((2 * 8, LANES), 1) // CG

    def one_tile(k, carry):
        tile = pl.program_id(0) * tiles + k
        at = pl.ds(pl.multiple_of(k * LANES, LANES), LANES)
        state = jnp.concatenate(
            [state_ref[pl.ds((a * all_tiles + tile) * 9, 8), :] for a in range(2)], 0
        )
        rights = []
        for part in split(state):
            part = part.astype(F32)
            rights.append(
                jnp.concatenate(
                    [jnp.where(lane_group == g, part, 0.0).astype(BF16) for g in range(GT)], 0
                )
            )
        high = high_ref[:, at]
        left = jnp.concatenate([high, low_ref[:, at], high], 1)
        right = jnp.concatenate([rights[0], rights[0], rights[1]], 0)
        out_ref[:, at] = local_ref[:, at] + dot(left, right)
        return carry

    lax.fori_loop(0, tiles, one_tile, 0, unroll=2)


def finish_kernel(factor_ref, a_ref, b_ref, c_ref, d_ref, out_ref):
    total = (a_ref[...] + b_ref[...]) + (c_ref[...] + d_ref[...])
    count = total.shape[0] // 2
    groups = out_ref.shape[1]
    pick = (iota((count, groups), 0) == iota((count, groups), 1) // GT).astype(F32)
    keep = iota((GT, CG, groups), 0) == iota((GT, CG, groups), 2) % GT
    for a in range(2):
        spread = lax.dot_general(
            total[a * count : (a + 1) * count],
            pick,
            (((0,), (0,)), ((), ())),
            precision=HIGHEST,
            preferred_element_type=F32,
        ).reshape(GT, CG, groups)
        cells = jnp.sum(jnp.where(keep, spread, 0.0), axis=0)
        out_ref[a * 8 : (a + 1) * 8, :] = cells[:8] * factor_ref[a * 8 : (a + 1) * 8, :]


def whole(shape):
    return pl.BlockSpec(shape, lambda *_: (0,) * len(shape))


def local(grad_out, inputs, residues, rates):
    _, rows, width = grad_out.shape
    modes, groups = residues.shape
    tiles = width // LANES
    shards = lax.axis_size(CTX)
    seqs = lax.axis_size("seq_x") * lax.axis_size("seq_core")
    steps = 4
    block = width // steps
    slab = pl.BlockSpec((rows, block), lambda q: (0, q))
    grad = grad_out[0]
    inp = inputs[0]
    vmem = pltpu.CompilerParams(vmem_limit_bytes=48 * 1024 * 1024)

    sent = pl.pallas_call(
        summary_kernel,
        grid=(steps,),
        in_specs=[whole((modes, groups)), slab, slab],
        out_specs=whole((shards * 17, LANES)),
        out_shape=jax.ShapeDtypeStruct((shards * 17, LANES), F32),
        compiler_params=vmem,
        name="summary",
    )(rates, grad, inp)
    got = lax.all_to_all(sent.reshape(shards, 1, 17 * LANES), CTX, 0, 0, tiled=True)

    amplitude = residues * jnp.sqrt(-jnp.expm1(-2.0 * rates) / modes)
    factor = jnp.sqrt(-jnp.expm1(-2.0 * rates) / float(seqs * shards * rows * (width // groups)))
    place = lax.axis_index(CTX)
    half = modes // 2
    own_rates = lax.dynamic_slice(
        rates, (place // tiles * half, place % tiles * GT), (half, GT)
    )
    decay = jnp.repeat(jnp.exp(-own_rates * rows), CG, axis=1)

    row = pl.BlockSpec((1, block), lambda q: (0, q))
    local_in, high, low = pl.pallas_call(
        local_kernel,
        grid=(steps,),
        in_specs=[whole((modes, groups)), whole((modes, groups)), row, row, slab],
        out_specs=[slab, slab, slab],
        out_shape=[
            jax.ShapeDtypeStruct((rows, width), F32),
            jax.ShapeDtypeStruct((rows, width), BF16),
            jax.ShapeDtypeStruct((rows, width), BF16),
        ],
        compiler_params=vmem,
        name="local",
        cost_estimate=pl.CostEstimate(
            flops=8 * 10**9, bytes_accessed=5 * 2**20, transcendentals=10**6
        ),
    )(rates, amplitude, rates.T.reshape(1, width), amplitude.T.reshape(1, width), grad)

    states = pl.pallas_call(
        scan_kernel,
        out_shape=jax.ShapeDtypeStruct((shards * 9, LANES), F32),
        name="scan",
    )(decay, got.reshape(shards * 17, LANES))
    back = lax.all_to_all(states.reshape(shards, 1, 9 * LANES), CTX, 0, 0, tiled=True)

    mine = back[:, 0, 8 * LANES :]
    others = [mine]
    for bits in (1, 2, 3):
        pairs = [(d, d ^ bits) for d in range(4)]
        others.append(lax.ppermute(mine, ("seq_x", "seq_core"), pairs))
    grad_in = pl.pallas_call(
        carry_kernel,
        grid=(steps,),
        in_specs=[whole((shards * 9, LANES)), slab, slab, slab],
        out_specs=slab,
        out_shape=jax.ShapeDtypeStruct((rows, width), F32),
        compiler_params=vmem,
        name="carry",
        cost_estimate=pl.CostEstimate(
            flops=8 * 10**8, bytes_accessed=7 * 2**20, transcendentals=0
        ),
    )(back.reshape(shards * 9, LANES), local_in, high, low)
    grad_res = pl.pallas_call(
        finish_kernel,
        out_shape=jax.ShapeDtypeStruct((modes, groups), F32),
        name="finish",
    )(factor, *others)
    return grad_in[None], grad_res


def solution(mesh):
    torus = Mesh(
        mesh.devices.reshape(2, 2, 2, 8, 4), ("seq_x", "seq_core", "ctx_0", "ctx_1", "ctx_2")
    )
    seq = ("seq_x", "seq_core")
    return jax.shard_map(
        local,
        mesh=torus,
        in_specs=(P(seq, CTX, None), P(seq, CTX, None), P(), P()),
        out_specs=(P(seq, CTX, None), P()),
        check_vma=False,
    )
```

```python
import functools

import jax
import jax.numpy as jnp
from jax import lax
from jax.experimental import pallas as pl
from jax.experimental.pallas import tpu as pltpu
from jax.sharding import Mesh
from jax.sharding import PartitionSpec as P

CTX = ("ctx_0", "ctx_1", "ctx_2")
LANES = 128
CG = 16
GT = LANES // CG
SUB = 16
STEPS = 4
F32 = jnp.float32
BF16 = jnp.bfloat16
HIGHEST = lax.Precision.HIGHEST


def iota(shape, dim):
    return lax.broadcasted_iota(jnp.int32, shape, dim)


def split(value):
    high = value.astype(BF16)
    return high, (value - high.astype(F32)).astype(BF16)


def dot(a, b, dims=((1,), (0,))):
    return lax.dot_general(a, b, (dims, ((), ())), preferred_element_type=F32)


def group_columns(table, first):
    groups = table.shape[1]
    turned = pltpu.roll(table, (groups - first) % groups, 1)
    return [jnp.broadcast_to(turned[:, g : g + 1], (table.shape[0], LANES)) for g in range(GT)]


def own_group(full, rows):
    group_of = iota((rows, LANES), 1) // CG
    kept = full[:rows]
    for g in range(1, GT):
        kept = jnp.where(group_of == g, full[g * rows : (g + 1) * rows], kept)
    return kept


def on_diagonal(part):
    group_of = iota(part.shape, 1) // CG
    zero = jnp.zeros_like(part)
    return jnp.concatenate([jnp.where(group_of == g, part, zero) for g in range(GT)], 0)


def windows(piece):
    shifted = [piece]
    for first in range(SUB, piece.shape[0], SUB):
        shifted.append(jnp.concatenate([piece[first:], jnp.zeros((first, LANES), BF16)], 0))
    return jnp.concatenate(shifted, 1)


def mode_rows(table):
    modes, groups = table.shape
    pick = (iota((modes, LANES), 0) == iota((modes, LANES), 1) % CG).astype(F32)
    spread = lax.dot_general(
        table, pick, (((0,), (0,)), ((), ())), precision=HIGHEST, preferred_element_type=F32
    ).reshape(groups // GT, GT, LANES)
    keep = iota((GT, LANES), 0) == iota((GT, LANES), 1) // CG
    return jnp.sum(jnp.where(keep[None], spread, 0.0), axis=1)


def summary_kernel(
    rates_hbm, grad_hbm, in_hbm, out_hbm, rates_ref, grad_ref, in_ref, sent_ref, pair_ref, sems, sent_sems
):
    rows, width = grad_ref.shape
    modes = rates_ref.shape[0]
    half = modes // 2
    all_tiles = width // LANES
    tiles = all_tiles // STEPS
    block = tiles * LANES
    chunk = tiles * 17
    loads = [pltpu.make_async_copy(rates_hbm, rates_ref, sems.at[0])]
    for q in range(STEPS):
        at = pl.ds(q * block, block)
        for i, (source, into) in enumerate(((grad_hbm, grad_ref), (in_hbm, in_ref))):
            loads.append(
                pltpu.make_async_copy(source.at[:, at], into.at[:, at], sems.at[1 + 2 * q + i])
            )
    for load in loads:
        load.start()
    pos = iota((modes, LANES), 1).astype(F32)
    step = iota((SUB, LANES), 0).astype(F32)
    later = iota((GT, SUB, LANES), 2) >= iota((GT, SUB, LANES), 1)
    later = later.reshape(GT * SUB, LANES)
    loads[0].wait()
    rates = rates_ref[...]
    rate_rows = mode_rows(rates)

    def pair_tile(tile):
        at = pl.ds(tile * LANES, LANES)
        inp = in_ref[:, at]
        left = jnp.concatenate(
            [on_diagonal(inp[i : i + SUB]) for i in range(0, rows, SUB)], 1
        )
        pairs = dot(left, windows(grad_ref[:, at]), ((1,), (1,)))
        high, low = split(jnp.where(later, pairs, 0.0))
        pair_ref[tile, :, :LANES] = high
        pair_ref[tile, :, LANES:] = low

    def one_tile(tile):
        at = pl.ds(tile * LANES, LANES)
        grad = grad_ref[:, at]
        inp = in_ref[:, at]
        columns = group_columns(rates, tile * GT)
        high, low = split(jnp.concatenate([jnp.exp(-r * pos) for r in columns], 0))
        left = jnp.concatenate([high, low], 1)
        summary = own_group(dot(left, jnp.concatenate([grad, grad], 0)), modes)
        tails = jnp.concatenate([jnp.exp(-r * (rows - pos)) for r in columns], 0)
        left = jnp.concatenate(split(tails), 1)
        tail = own_group(dot(left, jnp.concatenate([inp, inp], 0)), modes)
        pairs = pair_ref[tile]
        weighted = dot(
            jnp.concatenate([pairs, pairs[:, :LANES]], 1),
            jnp.concatenate([high, high, low], 1),
            ((1,), (1,)),
        )
        growth = jnp.exp(rate_rows[tile : tile + 1] * step)
        cells = jnp.sum(own_group(weighted, SUB) * growth, axis=0, keepdims=True)
        for a in range(2):
            base = (a * all_tiles + tile) * 17
            sent_ref[base : base + 8, :] = summary[a * half : (a + 1) * half]
            sent_ref[base + 8 : base + 16, :] = tail[a * half : (a + 1) * half]
            sent_ref[base + 16 : base + 17, :] = cells

    stores = []
    for q in range(STEPS):
        loads[1 + 2 * q].wait()
        loads[2 + 2 * q].wait()
        for tile in range(q * tiles, (q + 1) * tiles):
            pair_tile(tile)
        for tile in range(q * tiles, (q + 1) * tiles):
            one_tile(tile)
        for a in range(2):
            at = pl.ds((a * STEPS + q) * chunk, chunk)
            stores.append(
                pltpu.make_async_copy(
                    sent_ref.at[at], out_hbm.at[at], sent_sems.at[a * STEPS + q]
                )
            )
            stores[-1].start()
    for store in stores:
        store.wait()


def local_kernel(rates_ref, rate_row_ref, amp_row_ref, grad_ref, out_ref, weight_ref):
    rows = grad_ref.shape[0]
    modes = rates_ref.shape[0]
    tiles = grad_ref.shape[1] // LANES
    pos = iota((modes, LANES), 1).astype(F32)
    step = iota((SUB, LANES), 0).astype(F32)
    later = iota((GT, SUB, LANES), 2) >= iota((GT, SUB, LANES), 1)
    later = later.reshape(GT * SUB, LANES)
    to_end = (rows - iota((rows, LANES), 0)).astype(F32)

    def one_tile(k, carry):
        tile = pl.program_id(0) * tiles + k
        at = pl.ds(pl.multiple_of(k * LANES, LANES), LANES)
        grad = grad_ref[:, at]
        columns = group_columns(rates_ref[...], tile * GT)
        high, low = split(jnp.concatenate([jnp.exp(-r * pos) for r in columns], 0))
        amp_row = amp_row_ref[:, at]
        rate_row = rate_row_ref[:, at]
        grown = [on_diagonal(part) for part in split(amp_row * jnp.exp(rate_row * step))]
        kernel = dot(
            jnp.concatenate([grown[0], grown[1], grown[0]], 1),
            jnp.concatenate([high, high, low], 0),
        )
        left = jnp.concatenate(split(jnp.where(later, kernel, 0.0)), 1)
        wide = windows(grad)
        full = dot(left, jnp.concatenate([wide, wide], 0))
        for i in range(rows // SUB):
            out_ref[i * SUB : (i + 1) * SUB, at] = own_group(
                full[:, i * LANES : (i + 1) * LANES], SUB
            )
        high, low = split(amp_row * jnp.exp(-rate_row * to_end))
        weight_ref[:rows, at] = high
        weight_ref[rows:, at] = low
        return carry

    lax.fori_loop(0, tiles, one_tile, 0, unroll=8)


def scan_kernel(half_ref, decay_ref, in_ref, out_ref):
    shards = in_ref.shape[0] // 17
    decay = decay_ref[...]
    state = jnp.zeros((8, LANES), F32)
    total = jnp.zeros((8, LANES), F32)
    row = jnp.zeros((1, LANES), F32)
    for j in reversed(range(shards)):
        out_ref[9 * j : 9 * j + 8, :] = state
        total = total + in_ref[17 * j + 8 : 17 * j + 16, :] * state
        row = row + in_ref[17 * j + 16 : 17 * j + 17, :]
        state = in_ref[17 * j : 17 * j + 8, :] + decay * state
    same = iota((LANES, LANES), 0) // CG == iota((LANES, LANES), 1) // CG
    summed = lax.dot_general(
        total,
        same.astype(F32),
        (((1,), (0,)), ((), ())),
        precision=HIGHEST,
        preferred_element_type=F32,
    )
    place = iota((8, LANES), 1) % CG == iota((8, LANES), 0) + half_ref[0]
    row = row + jnp.sum(jnp.where(place, summed, 0.0), axis=0, keepdims=True)
    for j in range(shards):
        out_ref[9 * j + 8 : 9 * j + 9, :] = row


def carry_kernel(state_ref, local_ref, weight_ref, out_hbm, out_ref, sems):
    rows, width = out_ref.shape
    all_tiles = width // LANES
    block = width // STEPS
    stores = []
    for tile in range(all_tiles):
        at = pl.ds(tile * LANES, LANES)
        state = jnp.concatenate(
            [state_ref[pl.ds((a * all_tiles + tile) * 9, 8), :] for a in range(2)], 0
        )
        rights = [on_diagonal(part) for part in split(state)]
        high = weight_ref[:rows, at]
        left = jnp.concatenate([high, weight_ref[rows:, at], high], 1)
        right = jnp.concatenate([rights[0], rights[0], rights[1]], 0)
        out_ref[:, at] = local_ref[:, at] + dot(left, right)
        if (tile + 1) % (all_tiles // STEPS) == 0:
            q = tile // (all_tiles // STEPS)
            at = pl.ds(q * block, block)
            stores.append(
                pltpu.make_async_copy(out_ref.at[:, at], out_hbm.at[:, at], sems.at[q])
            )
            stores[-1].start()
    for store in stores:
        store.wait()


def finish_kernel(factor_ref, a_ref, b_ref, c_ref, d_ref, out_ref):
    total = (a_ref[...] + b_ref[...]) + (c_ref[...] + d_ref[...])
    count = total.shape[0] // 2
    modes, groups = out_ref.shape
    early = iota((count, LANES), 1) % CG < modes // 2
    total = jnp.where(early, total[:count], total[count:])
    pick = (iota((count, groups), 0) == iota((count, groups), 1) // GT).astype(F32)
    keep = iota((GT, CG, groups), 0) == iota((GT, CG, groups), 2) % GT
    spread = lax.dot_general(
        total, pick, (((0,), (0,)), ((), ())), precision=HIGHEST, preferred_element_type=F32
    ).reshape(GT, CG, groups)
    out_ref[...] = jnp.sum(jnp.where(keep, spread, 0.0), axis=0) * factor_ref[...]


def whole(shape):
    return pl.BlockSpec(shape, lambda *_: (0,) * len(shape))


def local(grad_out, inputs, residues, rates):
    _, rows, width = grad_out.shape
    modes, groups = residues.shape
    tiles = width // LANES
    shards = lax.axis_size(CTX)
    seqs = lax.axis_size("seq_x") * lax.axis_size("seq_core")
    block = width // STEPS
    slab = pl.BlockSpec((rows, block), lambda q: (0, q))
    anywhere = pl.BlockSpec(memory_space=pl.ANY)
    grad = grad_out[0]
    inp = inputs[0]
    full = pltpu.CompilerParams(vmem_limit_bytes=60 * 1024 * 1024)
    vmem = pltpu.CompilerParams(vmem_limit_bytes=16 * 1024 * 1024)
    small = pltpu.CompilerParams(vmem_limit_bytes=8 * 1024 * 1024)

    sent = pl.pallas_call(
        summary_kernel,
        in_specs=[anywhere, anywhere, anywhere],
        out_specs=anywhere,
        out_shape=jax.ShapeDtypeStruct((shards * 17, LANES), F32),
        scratch_shapes=[
            pltpu.VMEM((modes, groups), F32),
            pltpu.VMEM((rows, width), BF16),
            pltpu.VMEM((rows, width), BF16),
            pltpu.VMEM((shards * 17, LANES), F32),
            pltpu.VMEM((tiles, LANES, 2 * LANES), BF16),
            pltpu.SemaphoreType.DMA((1 + 2 * STEPS,)),
            pltpu.SemaphoreType.DMA((2 * STEPS,)),
        ],
        compiler_params=full,
        name="summary",
    )(rates, grad, inp)
    got = lax.all_to_all(sent.reshape(shards, 1, 17 * LANES), CTX, 0, 0, tiled=True)

    amplitude = residues * jnp.sqrt(-jnp.expm1(-2.0 * rates) / modes)
    factor = jnp.sqrt(-jnp.expm1(-2.0 * rates) / float(seqs * shards * rows * (width // groups)))
    place = lax.axis_index(CTX)
    half = modes // 2
    first_mode = place // tiles * half
    own_rates = lax.dynamic_slice(rates, (first_mode, place % tiles * GT), (half, GT))
    decay = jnp.repeat(jnp.exp(-own_rates * rows), CG, axis=1)

    row = pl.BlockSpec((1, block), lambda q: (0, q))
    local_in, weight = pl.pallas_call(
        local_kernel,
        grid=(STEPS,),
        in_specs=[whole((modes, groups)), row, row, slab],
        out_specs=[slab, pl.BlockSpec((2 * rows, block), lambda q: (0, q))],
        out_shape=[
            jax.ShapeDtypeStruct((rows, width), F32),
            jax.ShapeDtypeStruct((2 * rows, width), BF16),
        ],
        compiler_params=vmem,
        name="local",
        cost_estimate=pl.CostEstimate(
            flops=8 * 10**9, bytes_accessed=5 * 2**20, transcendentals=10**6
        ),
    )(rates, rates.T.reshape(1, width), amplitude.T.reshape(1, width), grad)

    got, local_in = lax.optimization_barrier((got, local_in))
    states = pl.pallas_call(
        scan_kernel,
        in_specs=[
            pl.BlockSpec(memory_space=pltpu.SMEM),
            whole((half, LANES)),
            whole((shards * 17, LANES)),
        ],
        out_shape=jax.ShapeDtypeStruct((shards * 9, LANES), F32),
        compiler_params=small,
        name="scan",
    )(first_mode[None], decay, got.reshape(shards * 17, LANES))
    back = lax.all_to_all(states.reshape(shards, 1, 9 * LANES), CTX, 0, 0, tiled=True)

    mine = back[:, 0, 8 * LANES :]
    others = [mine]
    for bits in (1, 2, 3):
        pairs = [(d, d ^ bits) for d in range(4)]
        others.append(lax.ppermute(mine, ("seq_x", "seq_core"), pairs))
    grad_in = pl.pallas_call(
        carry_kernel,
        in_specs=[whole((shards * 9, LANES)), whole((rows, width)), whole((2 * rows, width))],
        out_specs=anywhere,
        out_shape=jax.ShapeDtypeStruct((rows, width), F32),
        scratch_shapes=[pltpu.VMEM((rows, width), F32), pltpu.SemaphoreType.DMA((STEPS,))],
        compiler_params=vmem,
        name="carry",
        cost_estimate=pl.CostEstimate(
            flops=8 * 10**8, bytes_accessed=7 * 2**20, transcendentals=0
        ),
    )(back.reshape(shards * 9, LANES), local_in, weight)
    grad_res = pl.pallas_call(
        finish_kernel,
        out_shape=jax.ShapeDtypeStruct((modes, groups), F32),
        compiler_params=small,
        name="finish",
    )(factor, *others)
    return grad_in[None], grad_res


def solution(mesh):
    torus = Mesh(
        mesh.devices.reshape(2, 2, 2, 8, 4), ("seq_x", "seq_core", "ctx_0", "ctx_1", "ctx_2")
    )
    seq = ("seq_x", "seq_core")
    return jax.shard_map(
        local,
        mesh=torus,
        in_specs=(P(seq, CTX, None), P(seq, CTX, None), P(), P()),
        out_specs=(P(seq, CTX, None), P()),
        check_vma=False,
    )
```

```python
import jax
import jax.numpy as jnp
from jax import lax
from jax.experimental import pallas as pl
from jax.experimental.pallas import tpu as pltpu
from jax.sharding import Mesh
from jax.sharding import PartitionSpec as P

CTX = ("ctx_0", "ctx_1", "ctx_2")
LANES = 128
CG = 16
GT = LANES // CG
SUB = 16
STEPS = 4
HALVES = 2
F32 = jnp.float32
BF16 = jnp.bfloat16
HIGHEST = lax.Precision.HIGHEST


def iota(shape, dim):
    return lax.broadcasted_iota(jnp.int32, shape, dim)


def split(value):
    high = value.astype(BF16)
    return high, (value - high.astype(F32)).astype(BF16)


def dot(a, b, dims=((1,), (0,))):
    return lax.dot_general(a, b, (dims, ((), ())), preferred_element_type=F32)


def group_columns(table, first):
    groups = table.shape[1]
    turned = pltpu.roll(table, (groups - first) % groups, 1)
    return [jnp.broadcast_to(turned[:, g : g + 1], (table.shape[0], LANES)) for g in range(GT)]


def own_group(full, rows):
    group_of = iota((rows, LANES), 1) // CG
    kept = full[:rows]
    for g in range(1, GT):
        kept = jnp.where(group_of == g, full[g * rows : (g + 1) * rows], kept)
    return kept


def on_diagonal(part):
    group_of = iota(part.shape, 1) // CG
    zero = jnp.zeros_like(part)
    return jnp.concatenate([jnp.where(group_of == g, part, zero) for g in range(GT)], 0)


def windows(piece):
    shifted = [piece]
    for first in range(SUB, piece.shape[0], SUB):
        shifted.append(jnp.concatenate([piece[first:], jnp.zeros((first, LANES), BF16)], 0))
    return jnp.concatenate(shifted, 1)


def mode_row(columns):
    modes = columns[0].shape[0]
    ahead = iota((modes, LANES), 1) - iota((modes, LANES), 0)
    placed = jnp.where(ahead == 0, columns[0], 0.0)
    for g in range(1, GT):
        placed = jnp.where(ahead == g * CG, columns[g], placed)
    return jnp.sum(placed, axis=0, keepdims=True)


def summary_kernel(
    rates_hbm, grad_hbm, in_hbm, out_hbm, rates_ref, grad_ref, in_ref, sent_ref, pair_ref, sems, sent_sems
):
    rows, width = grad_ref.shape
    modes = rates_ref.shape[0]
    half = modes // 2
    all_tiles = width // LANES
    tiles = all_tiles // HALVES
    block = tiles * LANES
    chunk = tiles * 17
    loads = [pltpu.make_async_copy(rates_hbm, rates_ref, sems.at[0])]
    for q in range(HALVES):
        at = pl.ds(q * block, block)
        for i, (source, into) in enumerate(((grad_hbm, grad_ref), (in_hbm, in_ref))):
            loads.append(
                pltpu.make_async_copy(source.at[:, at], into.at[:, at], sems.at[1 + 2 * q + i])
            )
    for load in loads:
        load.start()
    pos = iota((modes, LANES), 1).astype(F32)
    step = iota((SUB, LANES), 0).astype(F32)
    later = iota((GT, SUB, LANES), 2) >= iota((GT, SUB, LANES), 1)
    later = later.reshape(GT * SUB, LANES)

    def pair_tile(tile):
        at = pl.ds(tile * LANES, LANES)
        inp = in_ref[:, at]
        left = jnp.concatenate(
            [on_diagonal(inp[i : i + SUB]) for i in range(0, rows, SUB)], 1
        )
        pairs = dot(left, windows(grad_ref[:, at]), ((1,), (1,)))
        high, low = split(jnp.where(later, pairs, 0.0))
        pair_ref[tile, :, :LANES] = high
        pair_ref[tile, :, LANES:] = low

    def one_tile(tile, rates):
        at = pl.ds(tile * LANES, LANES)
        grad = grad_ref[:, at]
        inp = in_ref[:, at]
        columns = group_columns(rates, tile * GT)
        high, low = split(jnp.concatenate([jnp.exp(-r * pos) for r in columns], 0))
        left = jnp.concatenate([high, low], 1)
        summary = own_group(dot(left, jnp.concatenate([grad, grad], 0)), modes)
        tails = jnp.concatenate([jnp.exp(-r * (rows - pos)) for r in columns], 0)
        left = jnp.concatenate(split(tails), 1)
        tail = own_group(dot(left, jnp.concatenate([inp, inp], 0)), modes)
        pairs = pair_ref[tile]
        weighted = dot(
            jnp.concatenate([pairs, pairs[:, :LANES]], 1),
            jnp.concatenate([high, high, low], 1),
            ((1,), (1,)),
        )
        growth = jnp.exp(mode_row(columns) * step)
        cells = jnp.sum(own_group(weighted, SUB) * growth, axis=0, keepdims=True)
        for a in range(2):
            base = (a * all_tiles + tile) * 17
            sent_ref[base : base + 8, :] = summary[a * half : (a + 1) * half]
            sent_ref[base + 8 : base + 16, :] = tail[a * half : (a + 1) * half]
            sent_ref[base + 16 : base + 17, :] = cells

    def arrived(q):
        loads[1 + 2 * q].wait()
        loads[2 + 2 * q].wait()

    def of_step(q):
        return range(q * tiles, (q + 1) * tiles)

    arrived(0)
    for tile in of_step(0):
        pair_tile(tile)
    loads[0].wait()
    rates = rates_ref[...]
    stores = []
    for q in range(HALVES):
        if q + 1 < HALVES:
            arrived(q + 1)
            for tile in of_step(q + 1):
                pair_tile(tile)
        for tile in of_step(q):
            one_tile(tile, rates)
        for a in range(2):
            at = pl.ds((a * HALVES + q) * chunk, chunk)
            stores.append(
                pltpu.make_async_copy(
                    sent_ref.at[at], out_hbm.at[at], sent_sems.at[a * HALVES + q]
                )
            )
            stores[-1].start()
    for store in stores:
        store.wait()


def local_kernel(rates_ref, rate_row_ref, amp_row_ref, grad_ref, out_ref, near_ref, far_ref):
    rows = grad_ref.shape[0]
    modes = rates_ref.shape[0]
    tiles = grad_ref.shape[1] // LANES
    pos = iota((modes, LANES), 1).astype(F32)
    step = iota((SUB, LANES), 0).astype(F32)
    later = iota((GT, SUB, LANES), 2) >= iota((GT, SUB, LANES), 1)
    later = later.reshape(GT * SUB, LANES)
    blocks = rows // SUB
    to_next = (SUB - iota((SUB, LANES), 0)).astype(F32)
    to_end = (SUB * (blocks - 1 - iota((blocks, LANES), 0))).astype(F32)

    def one_tile(k, carry):
        tile = pl.program_id(0) * tiles + k
        at = pl.ds(pl.multiple_of(k * LANES, LANES), LANES)
        grad = grad_ref[:, at]
        columns = group_columns(rates_ref[...], tile * GT)
        high, low = split(jnp.concatenate([jnp.exp(-r * pos) for r in columns], 0))
        amp_row = amp_row_ref[:, at]
        rate_row = rate_row_ref[:, at]
        grown = [on_diagonal(part) for part in split(amp_row * jnp.exp(rate_row * step))]
        kernel = dot(
            jnp.concatenate([grown[0], grown[1], grown[0]], 1),
            jnp.concatenate([high, high, low], 0),
        )
        left = jnp.concatenate(split(jnp.where(later, kernel, 0.0)), 1)
        wide = windows(grad)
        full = dot(left, jnp.concatenate([wide, wide], 0))
        for i in range(rows // SUB):
            out_ref[i * SUB : (i + 1) * SUB, at] = own_group(
                full[:, i * LANES : (i + 1) * LANES], SUB
            )
        near_ref[:, at] = amp_row * jnp.exp(-rate_row * to_next)
        far_ref[:, at] = jnp.exp(-rate_row * to_end)
        return carry

    lax.fori_loop(0, tiles, one_tile, 0, unroll=8)


def scan_kernel(half_ref, decay_ref, in_ref, out_ref):
    shards = in_ref.shape[0] // 17
    decay = decay_ref[...]
    state = jnp.zeros((8, LANES), F32)
    total = jnp.zeros((8, LANES), F32)
    row = jnp.zeros((1, LANES), F32)
    for j in reversed(range(shards)):
        out_ref[9 * j : 9 * j + 8, :] = state
        total = total + in_ref[17 * j + 8 : 17 * j + 16, :] * state
        row = row + in_ref[17 * j + 16 : 17 * j + 17, :]
        state = in_ref[17 * j : 17 * j + 8, :] + decay * state
    same = iota((LANES, LANES), 0) // CG == iota((LANES, LANES), 1) // CG
    summed = lax.dot_general(
        total,
        same.astype(F32),
        (((1,), (0,)), ((), ())),
        precision=HIGHEST,
        preferred_element_type=F32,
    )
    place = iota((8, LANES), 1) % CG == iota((8, LANES), 0) + half_ref[0]
    row = row + jnp.sum(jnp.where(place, summed, 0.0), axis=0, keepdims=True)
    for j in range(shards):
        out_ref[9 * j + 8 : 9 * j + 9, :] = row


def carry_kernel(state_ref, local_ref, near_ref, far_ref, out_hbm, out_ref, sems):
    rows, width = out_ref.shape
    all_tiles = width // LANES
    block = width // STEPS
    stores = []
    for tile in range(all_tiles):
        at = pl.ds(tile * LANES, LANES)
        state = jnp.concatenate(
            [state_ref[pl.ds((a * all_tiles + tile) * 9, 8), :] for a in range(2)], 0
        )
        rights = [on_diagonal(part) for part in split(state)]
        near = near_ref[:, at]
        far = far_ref[:, at]
        high, low = split(
            jnp.concatenate([near * far[i : i + 1] for i in range(rows // SUB)], 0)
        )
        left = jnp.concatenate([high, low, high], 1)
        right = jnp.concatenate([rights[0], rights[0], rights[1]], 0)
        out_ref[:, at] = local_ref[:, at] + dot(left, right)
        if (tile + 1) % (all_tiles // STEPS) == 0:
            q = tile // (all_tiles // STEPS)
            at = pl.ds(q * block, block)
            stores.append(
                pltpu.make_async_copy(out_ref.at[:, at], out_hbm.at[:, at], sems.at[q])
            )
            stores[-1].start()
    for store in stores:
        store.wait()


def finish_kernel(factor_ref, a_ref, b_ref, c_ref, d_ref, out_ref):
    total = (a_ref[...] + b_ref[...]) + (c_ref[...] + d_ref[...])
    count = total.shape[0] // 2
    modes, groups = out_ref.shape
    early = iota((count, LANES), 1) % CG < modes // 2
    total = jnp.where(early, total[:count], total[count:])
    pick = (iota((count, groups), 0) == iota((count, groups), 1) // GT).astype(F32)
    keep = iota((GT, CG, groups), 0) == iota((GT, CG, groups), 2) % GT
    spread = lax.dot_general(
        total, pick, (((0,), (0,)), ((), ())), precision=HIGHEST, preferred_element_type=F32
    ).reshape(GT, CG, groups)
    out_ref[...] = jnp.sum(jnp.where(keep, spread, 0.0), axis=0) * factor_ref[...]


def whole(shape):
    return pl.BlockSpec(shape, lambda *_: (0,) * len(shape))


def local(grad_out, inputs, residues, rates):
    _, rows, width = grad_out.shape
    modes, groups = residues.shape
    tiles = width // LANES
    shards = lax.axis_size(CTX)
    seqs = lax.axis_size("seq_x") * lax.axis_size("seq_core")
    block = width // STEPS
    slab = pl.BlockSpec((rows, block), lambda q: (0, q))
    anywhere = pl.BlockSpec(memory_space=pl.ANY)
    grad = grad_out[0]
    inp = inputs[0]
    full = pltpu.CompilerParams(vmem_limit_bytes=60 * 1024 * 1024)
    vmem = pltpu.CompilerParams(vmem_limit_bytes=16 * 1024 * 1024)
    small = pltpu.CompilerParams(vmem_limit_bytes=8 * 1024 * 1024)

    sent = pl.pallas_call(
        summary_kernel,
        in_specs=[anywhere, anywhere, anywhere],
        out_specs=anywhere,
        out_shape=jax.ShapeDtypeStruct((shards * 17, LANES), F32),
        scratch_shapes=[
            pltpu.VMEM((modes, groups), F32),
            pltpu.VMEM((rows, width), BF16),
            pltpu.VMEM((rows, width), BF16),
            pltpu.VMEM((shards * 17, LANES), F32),
            pltpu.VMEM((tiles, LANES, 2 * LANES), BF16),
            pltpu.SemaphoreType.DMA((1 + 2 * HALVES,)),
            pltpu.SemaphoreType.DMA((2 * HALVES,)),
        ],
        compiler_params=full,
        name="summary",
    )(rates, grad, inp)
    got = lax.all_to_all(sent.reshape(shards, 1, 17 * LANES), CTX, 0, 0, tiled=True)

    amplitude = residues * jnp.sqrt(-jnp.expm1(-2.0 * rates) / modes)
    factor = jnp.sqrt(-jnp.expm1(-2.0 * rates) / float(seqs * shards * rows * (width // groups)))
    place = lax.axis_index(CTX)
    half = modes // 2
    first_mode = place // tiles * half
    own_rates = lax.dynamic_slice(rates, (first_mode, place % tiles * GT), (half, GT))
    decay = jnp.repeat(jnp.exp(-own_rates * rows), CG, axis=1)

    row = pl.BlockSpec((1, block), lambda q: (0, q))
    local_in, near, far = pl.pallas_call(
        local_kernel,
        grid=(STEPS,),
        in_specs=[whole((modes, groups)), row, row, slab],
        out_specs=[
            slab,
            pl.BlockSpec((SUB, block), lambda q: (0, q)),
            pl.BlockSpec((rows // SUB, block), lambda q: (0, q)),
        ],
        out_shape=[
            jax.ShapeDtypeStruct((rows, width), F32),
            jax.ShapeDtypeStruct((SUB, width), F32),
            jax.ShapeDtypeStruct((rows // SUB, width), F32),
        ],
        compiler_params=vmem,
        name="local",
        cost_estimate=pl.CostEstimate(
            flops=8 * 10**9, bytes_accessed=5 * 2**20, transcendentals=10**6
        ),
    )(rates, rates.T.reshape(1, width), amplitude.T.reshape(1, width), grad)

    got, local_in = lax.optimization_barrier((got, local_in))
    states = pl.pallas_call(
        scan_kernel,
        in_specs=[
            pl.BlockSpec(memory_space=pltpu.SMEM),
            whole((half, LANES)),
            whole((shards * 17, LANES)),
        ],
        out_shape=jax.ShapeDtypeStruct((shards * 9, LANES), F32),
        compiler_params=small,
        name="scan",
    )(first_mode[None], decay, got.reshape(shards * 17, LANES))
    back = lax.all_to_all(states.reshape(shards, 1, 9 * LANES), CTX, 0, 0, tiled=True)

    mine = back[:, 0, 8 * LANES :]
    others = [mine]
    for bits in (1, 2, 3):
        pairs = [(d, d ^ bits) for d in range(4)]
        others.append(lax.ppermute(mine, ("seq_x", "seq_core"), pairs))
    grad_in = pl.pallas_call(
        carry_kernel,
        in_specs=[
            whole((shards * 9, LANES)),
            whole((rows, width)),
            whole((SUB, width)),
            whole((rows // SUB, width)),
        ],
        out_specs=anywhere,
        out_shape=jax.ShapeDtypeStruct((rows, width), F32),
        scratch_shapes=[pltpu.VMEM((rows, width), F32), pltpu.SemaphoreType.DMA((STEPS,))],
        compiler_params=vmem,
        name="carry",
        cost_estimate=pl.CostEstimate(
            flops=8 * 10**8, bytes_accessed=7 * 2**20, transcendentals=0
        ),
    )(back.reshape(shards * 9, LANES), local_in, near, far)
    grad_res = pl.pallas_call(
        finish_kernel,
        out_shape=jax.ShapeDtypeStruct((modes, groups), F32),
        compiler_params=small,
        name="finish",
    )(factor, *others)
    return grad_in[None], grad_res


def solution(mesh):
    torus = Mesh(
        mesh.devices.reshape(2, 2, 2, 8, 4), ("seq_x", "seq_core", "ctx_0", "ctx_1", "ctx_2")
    )
    seq = ("seq_x", "seq_core")
    return jax.shard_map(
        local,
        mesh=torus,
        in_specs=(P(seq, CTX, None), P(seq, CTX, None), P(), P()),
        out_specs=(P(seq, CTX, None), P()),
        check_vma=False,
    )
```

```python
import jax
import jax.numpy as jnp
from jax import lax
from jax.experimental import pallas as pl
from jax.experimental.pallas import tpu as pltpu
from jax.sharding import Mesh
from jax.sharding import PartitionSpec as P

CTX = ("ctx_0", "ctx_1", "ctx_2")
LANES = 128
CG = 16
GT = LANES // CG
SUB = 16
STEPS = 4
HALVES = 2
F32 = jnp.float32
BF16 = jnp.bfloat16


def iota(shape, dim):
    return lax.broadcasted_iota(jnp.int32, shape, dim)


def split(value):
    high = value.astype(BF16)
    return high, (value - high.astype(F32)).astype(BF16)


def dot(a, b, dims=((1,), (0,))):
    return lax.dot_general(a, b, (dims, ((), ())), preferred_element_type=F32)


def group_columns(table, first):
    groups = table.shape[1]
    turned = pltpu.roll(table, (groups - first) % groups, 1)
    return [jnp.broadcast_to(turned[:, g : g + 1], (table.shape[0], LANES)) for g in range(GT)]


def own_group(full, rows):
    group_of = iota((rows, LANES), 1) // CG
    kept = full[:rows]
    for g in range(1, GT):
        kept = jnp.where(group_of == g, full[g * rows : (g + 1) * rows], kept)
    return kept


def on_diagonal(part):
    group_of = iota(part.shape, 1) // CG
    zero = jnp.zeros_like(part)
    return jnp.concatenate([jnp.where(group_of == g, part, zero) for g in range(GT)], 0)


def windows(piece):
    shifted = [piece]
    for first in range(SUB, piece.shape[0], SUB):
        shifted.append(jnp.concatenate([piece[first:], jnp.zeros((first, LANES), BF16)], 0))
    return jnp.concatenate(shifted, 1)


def mode_row(columns):
    modes = columns[0].shape[0]
    ahead = iota((modes, LANES), 1) - iota((modes, LANES), 0)
    placed = jnp.where(ahead == 0, columns[0], 0.0)
    for g in range(1, GT):
        placed = jnp.where(ahead == g * CG, columns[g], placed)
    return jnp.sum(placed, axis=0, keepdims=True)


def summary_kernel(
    rates_hbm, grad_hbm, in_hbm, out_hbm, rates_ref, grad_ref, in_ref, sent_ref, pair_ref, sems, sent_sems
):
    rows, width = grad_ref.shape
    modes = rates_ref.shape[0]
    half = modes // 2
    all_tiles = width // LANES
    tiles = all_tiles // HALVES
    block = tiles * LANES
    chunk = tiles * 17
    loads = [pltpu.make_async_copy(rates_hbm, rates_ref, sems.at[0])]
    for q in range(HALVES):
        at = pl.ds(q * block, block)
        for i, (source, into) in enumerate(((grad_hbm, grad_ref), (in_hbm, in_ref))):
            loads.append(
                pltpu.make_async_copy(source.at[:, at], into.at[:, at], sems.at[1 + 2 * q + i])
            )
    for load in loads:
        load.start()
    pos = iota((modes, LANES), 1).astype(F32)
    step = iota((SUB, LANES), 0).astype(F32)
    later = iota((GT, SUB, LANES), 2) >= iota((GT, SUB, LANES), 1)
    later = later.reshape(GT * SUB, LANES)

    def pair_tile(tile):
        at = pl.ds(tile * LANES, LANES)
        inp = in_ref[:, at]
        left = jnp.concatenate(
            [on_diagonal(inp[i : i + SUB]) for i in range(0, rows, SUB)], 1
        )
        pairs = dot(left, windows(grad_ref[:, at]), ((1,), (1,)))
        high, low = split(jnp.where(later, pairs, 0.0))
        pair_ref[tile, :, :LANES] = high
        pair_ref[tile, :, LANES:] = low

    def one_tile(tile, rates):
        at = pl.ds(tile * LANES, LANES)
        grad = grad_ref[:, at]
        inp = in_ref[:, at]
        columns = group_columns(rates, tile * GT)
        high, low = split(jnp.concatenate([jnp.exp(-r * pos) for r in columns], 0))
        left = jnp.concatenate([high, low], 1)
        summary = own_group(dot(left, jnp.concatenate([grad, grad], 0)), modes)
        tails = jnp.concatenate([jnp.exp(-r * (rows - pos)) for r in columns], 0)
        left = jnp.concatenate(split(tails), 1)
        tail = own_group(dot(left, jnp.concatenate([inp, inp], 0)), modes)
        pairs = pair_ref[tile]
        weighted = dot(
            jnp.concatenate([pairs, pairs[:, :LANES]], 1),
            jnp.concatenate([high, high, low], 1),
            ((1,), (1,)),
        )
        growth = jnp.exp(mode_row(columns) * step)
        cells = jnp.sum(own_group(weighted, SUB) * growth, axis=0, keepdims=True)
        for a in range(2):
            base = (a * all_tiles + tile) * 17
            sent_ref[base : base + 8, :] = summary[a * half : (a + 1) * half]
            sent_ref[base + 8 : base + 16, :] = tail[a * half : (a + 1) * half]
            sent_ref[base + 16 : base + 17, :] = cells

    def arrived(q):
        loads[1 + 2 * q].wait()
        loads[2 + 2 * q].wait()

    def of_step(q):
        return range(q * tiles, (q + 1) * tiles)

    arrived(0)
    for tile in of_step(0):
        pair_tile(tile)
    loads[0].wait()
    rates = rates_ref[...]
    stores = []
    for q in range(HALVES):
        if q + 1 < HALVES:
            arrived(q + 1)
            for tile in of_step(q + 1):
                pair_tile(tile)
        for tile in of_step(q):
            one_tile(tile, rates)
        for a in range(2):
            at = pl.ds((a * HALVES + q) * chunk, chunk)
            stores.append(
                pltpu.make_async_copy(
                    sent_ref.at[at], out_hbm.at[at], sent_sems.at[a * HALVES + q]
                )
            )
            stores[-1].start()
    for store in stores:
        store.wait()


def local_kernel(rates_ref, rate_row_ref, amp_row_ref, grad_ref, out_ref, near_ref, far_ref):
    rows = grad_ref.shape[0]
    modes = rates_ref.shape[0]
    tiles = grad_ref.shape[1] // LANES
    pos = iota((modes, LANES), 1).astype(F32)
    step = iota((SUB, LANES), 0).astype(F32)
    later = iota((GT, SUB, LANES), 2) >= iota((GT, SUB, LANES), 1)
    later = later.reshape(GT * SUB, LANES)
    blocks = rows // SUB
    to_next = (SUB - iota((SUB, LANES), 0)).astype(F32)
    to_end = (SUB * (blocks - 1 - iota((blocks, LANES), 0))).astype(F32)

    def one_tile(k, carry):
        tile = pl.program_id(0) * tiles + k
        at = pl.ds(pl.multiple_of(k * LANES, LANES), LANES)
        grad = grad_ref[:, at]
        columns = group_columns(rates_ref[...], tile * GT)
        high, low = split(jnp.concatenate([jnp.exp(-r * pos) for r in columns], 0))
        amp_row = amp_row_ref[:, at]
        rate_row = rate_row_ref[:, at]
        grown = [on_diagonal(part) for part in split(amp_row * jnp.exp(rate_row * step))]
        kernel = dot(
            jnp.concatenate([grown[0], grown[1], grown[0]], 1),
            jnp.concatenate([high, high, low], 0),
        )
        left = jnp.concatenate(split(jnp.where(later, kernel, 0.0)), 1)
        wide = windows(grad)
        full = dot(left, jnp.concatenate([wide, wide], 0))
        for i in range(rows // SUB):
            out_ref[i * SUB : (i + 1) * SUB, at] = own_group(
                full[:, i * LANES : (i + 1) * LANES], SUB
            )
        near_ref[:, at] = amp_row * jnp.exp(-rate_row * to_next)
        far_ref[:, at] = jnp.exp(-rate_row * to_end)
        return carry

    lax.fori_loop(0, tiles, one_tile, 0, unroll=8)


def scan_kernel(half_ref, decay_ref, in_ref, out_ref):
    shards = in_ref.shape[0] // 17
    decay = decay_ref[...]
    state = jnp.zeros((8, LANES), F32)
    total = jnp.zeros((8, LANES), F32)
    row = jnp.zeros((1, LANES), F32)
    for j in reversed(range(shards)):
        out_ref[9 * j : 9 * j + 8, :] = state
        total = total + in_ref[17 * j + 8 : 17 * j + 16, :] * state
        row = row + in_ref[17 * j + 16 : 17 * j + 17, :]
        state = in_ref[17 * j : 17 * j + 8, :] + decay * state
    same = iota((2 * LANES, LANES), 0) // CG % GT == iota((2 * LANES, LANES), 1) // CG
    summed = dot(jnp.concatenate(split(total), 1), same.astype(F32).astype(BF16))
    place = iota((8, LANES), 1) % CG == iota((8, LANES), 0) + half_ref[0]
    row = row + jnp.sum(jnp.where(place, summed, 0.0), axis=0, keepdims=True)
    for j in range(shards):
        out_ref[9 * j + 8 : 9 * j + 9, :] = row


def carry_kernel(state_ref, local_ref, near_ref, far_ref, out_hbm, out_ref, sems):
    rows, width = out_ref.shape
    all_tiles = width // LANES
    block = width // STEPS
    stores = []
    for tile in range(all_tiles):
        at = pl.ds(tile * LANES, LANES)
        state = jnp.concatenate(
            [state_ref[pl.ds((a * all_tiles + tile) * 9, 8), :] for a in range(2)], 0
        )
        rights = [on_diagonal(part) for part in split(state)]
        near = near_ref[:, at]
        far = far_ref[:, at]
        high, low = split(
            jnp.concatenate([near * far[i : i + 1] for i in range(rows // SUB)], 0)
        )
        left = jnp.concatenate([high, low, high], 1)
        right = jnp.concatenate([rights[0], rights[0], rights[1]], 0)
        out_ref[:, at] = local_ref[:, at] + dot(left, right)
        if (tile + 1) % (all_tiles // STEPS) == 0:
            q = tile // (all_tiles // STEPS)
            at = pl.ds(q * block, block)
            stores.append(
                pltpu.make_async_copy(out_ref.at[:, at], out_hbm.at[:, at], sems.at[q])
            )
            stores[-1].start()
    for store in stores:
        store.wait()


def finish_kernel(factor_ref, a_ref, b_ref, c_ref, d_ref, out_ref):
    total = (a_ref[...] + b_ref[...]) + (c_ref[...] + d_ref[...])
    count = total.shape[0] // 2
    modes, groups = out_ref.shape
    early = iota((count, LANES), 1) % CG < modes // 2
    total = jnp.where(early, total[:count], total[count:])
    pick = iota((2 * count, groups), 0) % count == iota((2 * count, groups), 1) // GT
    keep = iota((GT, CG, groups), 0) == iota((GT, CG, groups), 2) % GT
    spread = dot(
        jnp.concatenate(split(total), 0), pick.astype(F32).astype(BF16), ((0,), (0,))
    ).reshape(GT, CG, groups)
    out_ref[...] = jnp.sum(jnp.where(keep, spread, 0.0), axis=0) * factor_ref[...]


def whole(shape):
    return pl.BlockSpec(shape, lambda *_: (0,) * len(shape))


def local(grad_out, inputs, residues, rates):
    _, rows, width = grad_out.shape
    modes, groups = residues.shape
    tiles = width // LANES
    shards = lax.axis_size(CTX)
    seqs = lax.axis_size("seq_x") * lax.axis_size("seq_core")
    block = width // STEPS
    slab = pl.BlockSpec((rows, block), lambda q: (0, q))
    anywhere = pl.BlockSpec(memory_space=pl.ANY)
    grad = grad_out[0]
    inp = inputs[0]
    full = pltpu.CompilerParams(vmem_limit_bytes=60 * 1024 * 1024)
    vmem = pltpu.CompilerParams(vmem_limit_bytes=16 * 1024 * 1024)
    small = pltpu.CompilerParams(vmem_limit_bytes=8 * 1024 * 1024)

    sent = pl.pallas_call(
        summary_kernel,
        in_specs=[anywhere, anywhere, anywhere],
        out_specs=anywhere,
        out_shape=jax.ShapeDtypeStruct((shards * 17, LANES), F32),
        scratch_shapes=[
            pltpu.VMEM((modes, groups), F32),
            pltpu.VMEM((rows, width), BF16),
            pltpu.VMEM((rows, width), BF16),
            pltpu.VMEM((shards * 17, LANES), F32),
            pltpu.VMEM((tiles, LANES, 2 * LANES), BF16),
            pltpu.SemaphoreType.DMA((1 + 2 * HALVES,)),
            pltpu.SemaphoreType.DMA((2 * HALVES,)),
        ],
        compiler_params=full,
        name="summary",
    )(rates, grad, inp)
    got = lax.all_to_all(sent.reshape(shards, 1, 17 * LANES), CTX, 0, 0, tiled=True)

    amplitude = residues * jnp.sqrt(-jnp.expm1(-2.0 * rates) / modes)
    factor = jnp.sqrt(-jnp.expm1(-2.0 * rates) / float(seqs * shards * rows * (width // groups)))
    place = lax.axis_index(CTX)
    half = modes // 2
    first_mode = place // tiles * half
    own_rates = lax.dynamic_slice(rates, (first_mode, place % tiles * GT), (half, GT))
    decay = jnp.repeat(jnp.exp(-own_rates * rows), CG, axis=1)

    row = pl.BlockSpec((1, block), lambda q: (0, q))
    local_in, near, far = pl.pallas_call(
        local_kernel,
        grid=(STEPS,),
        in_specs=[whole((modes, groups)), row, row, slab],
        out_specs=[
            slab,
            pl.BlockSpec((SUB, block), lambda q: (0, q)),
            pl.BlockSpec((rows // SUB, block), lambda q: (0, q)),
        ],
        out_shape=[
            jax.ShapeDtypeStruct((rows, width), F32),
            jax.ShapeDtypeStruct((SUB, width), F32),
            jax.ShapeDtypeStruct((rows // SUB, width), F32),
        ],
        compiler_params=vmem,
        name="local",
        cost_estimate=pl.CostEstimate(
            flops=8 * 10**9, bytes_accessed=5 * 2**20, transcendentals=10**6
        ),
    )(rates, rates.T.reshape(1, width), amplitude.T.reshape(1, width), grad)

    got, local_in = lax.optimization_barrier((got, local_in))
    states = pl.pallas_call(
        scan_kernel,
        in_specs=[
            pl.BlockSpec(memory_space=pltpu.SMEM),
            whole((half, LANES)),
            whole((shards * 17, LANES)),
        ],
        out_shape=jax.ShapeDtypeStruct((shards * 9, LANES), F32),
        compiler_params=small,
        name="scan",
    )(first_mode[None], decay, got.reshape(shards * 17, LANES))
    back = lax.all_to_all(states.reshape(shards, 1, 9 * LANES), CTX, 0, 0, tiled=True)

    mine = back[:, 0, 8 * LANES :]
    others = [mine]
    for bits in (1, 2, 3):
        pairs = [(d, d ^ bits) for d in range(4)]
        others.append(lax.ppermute(mine, ("seq_x", "seq_core"), pairs))
    grad_in = pl.pallas_call(
        carry_kernel,
        in_specs=[
            whole((shards * 9, LANES)),
            whole((rows, width)),
            whole((SUB, width)),
            whole((rows // SUB, width)),
        ],
        out_specs=anywhere,
        out_shape=jax.ShapeDtypeStruct((rows, width), F32),
        scratch_shapes=[pltpu.VMEM((rows, width), F32), pltpu.SemaphoreType.DMA((STEPS,))],
        compiler_params=vmem,
        name="carry",
        cost_estimate=pl.CostEstimate(
            flops=8 * 10**8, bytes_accessed=7 * 2**20, transcendentals=0
        ),
    )(back.reshape(shards * 9, LANES), local_in, near, far)
    grad_res = pl.pallas_call(
        finish_kernel,
        out_shape=jax.ShapeDtypeStruct((modes, groups), F32),
        compiler_params=small,
        name="finish",
    )(factor, *others)
    return grad_in[None], grad_res


def solution(mesh):
    torus = Mesh(
        mesh.devices.reshape(2, 2, 2, 8, 4), ("seq_x", "seq_core", "ctx_0", "ctx_1", "ctx_2")
    )
    seq = ("seq_x", "seq_core")
    return jax.shard_map(
        local,
        mesh=torus,
        in_specs=(P(seq, CTX, None), P(seq, CTX, None), P(), P()),
        out_specs=(P(seq, CTX, None), P()),
        check_vma=False,
    )
```

```python
import jax
import jax.numpy as jnp
from jax import lax
from jax.experimental import pallas as pl
from jax.experimental.pallas import tpu as pltpu
from jax.sharding import Mesh
from jax.sharding import PartitionSpec as P

CTX = ("ctx_0", "ctx_1", "ctx_2")
LANES = 128
CG = 16
GT = LANES // CG
SUB = 16
STEPS = 4
HALVES = 2
PIECES = 8
F32 = jnp.float32
BF16 = jnp.bfloat16


def iota(shape, dim):
    return lax.broadcasted_iota(jnp.int32, shape, dim)


def split(value):
    high = value.astype(BF16)
    return high, (value - high.astype(F32)).astype(BF16)


def dot(a, b, dims=((1,), (0,))):
    return lax.dot_general(a, b, (dims, ((), ())), preferred_element_type=F32)


def group_columns(table, first):
    groups = table.shape[1]
    turned = pltpu.roll(table, (groups - first) % groups, 1)
    return [jnp.broadcast_to(turned[:, g : g + 1], (table.shape[0], LANES)) for g in range(GT)]


def own_group(full, rows):
    group_of = iota((rows, LANES), 1) // CG
    kept = full[:rows]
    for g in range(1, GT):
        kept = jnp.where(group_of == g, full[g * rows : (g + 1) * rows], kept)
    return kept


def on_diagonal(part):
    group_of = iota(part.shape, 1) // CG
    zero = jnp.zeros_like(part)
    return jnp.concatenate([jnp.where(group_of == g, part, zero) for g in range(GT)], 0)


def windows(piece):
    shifted = [piece]
    for first in range(SUB, piece.shape[0], SUB):
        shifted.append(jnp.concatenate([piece[first:], jnp.zeros((first, LANES), BF16)], 0))
    return jnp.concatenate(shifted, 1)


def mode_row(columns):
    modes = columns[0].shape[0]
    ahead = iota((modes, LANES), 1) - iota((modes, LANES), 0)
    placed = jnp.where(ahead == 0, columns[0], 0.0)
    for g in range(1, GT):
        placed = jnp.where(ahead == g * CG, columns[g], placed)
    return jnp.sum(placed, axis=0, keepdims=True)


def summary_kernel(
    rates_hbm, grad_hbm, in_hbm, out_hbm, rates_ref, grad_ref, in_ref, sent_ref, pair_ref, sems, sent_sems
):
    rows, width = grad_ref.shape
    modes = rates_ref.shape[0]
    half = modes // 2
    all_tiles = width // LANES
    tiles = all_tiles // HALVES
    block = tiles * LANES
    chunk = tiles * 17
    loads = [pltpu.make_async_copy(rates_hbm, rates_ref, sems.at[0])]
    for q in range(HALVES):
        at = pl.ds(q * block, block)
        for i, (source, into) in enumerate(((grad_hbm, grad_ref), (in_hbm, in_ref))):
            loads.append(
                pltpu.make_async_copy(source.at[:, at], into.at[:, at], sems.at[1 + 2 * q + i])
            )
    for load in loads:
        load.start()
    pos = iota((modes, LANES), 1).astype(F32)
    step = iota((SUB, LANES), 0).astype(F32)
    later = iota((GT, SUB, LANES), 2) >= iota((GT, SUB, LANES), 1)
    later = later.reshape(GT * SUB, LANES)

    def pair_tile(tile):
        at = pl.ds(tile * LANES, LANES)
        inp = in_ref[:, at]
        left = jnp.concatenate(
            [on_diagonal(inp[i : i + SUB]) for i in range(0, rows, SUB)], 1
        )
        pairs = dot(left, windows(grad_ref[:, at]), ((1,), (1,)))
        high, low = split(jnp.where(later, pairs, 0.0))
        pair_ref[tile, :, :LANES] = high
        pair_ref[tile, :, LANES:] = low

    def one_tile(tile, rates):
        at = pl.ds(tile * LANES, LANES)
        grad = grad_ref[:, at]
        inp = in_ref[:, at]
        columns = group_columns(rates, tile * GT)
        high, low = split(jnp.concatenate([jnp.exp(-r * pos) for r in columns], 0))
        left = jnp.concatenate([high, low], 1)
        summary = own_group(dot(left, jnp.concatenate([grad, grad], 0)), modes)
        tails = jnp.concatenate([jnp.exp(-r * (rows - pos)) for r in columns], 0)
        left = jnp.concatenate(split(tails), 1)
        tail = own_group(dot(left, jnp.concatenate([inp, inp], 0)), modes)
        pairs = pair_ref[tile]
        weighted = dot(
            jnp.concatenate([pairs, pairs[:, :LANES]], 1),
            jnp.concatenate([high, high, low], 1),
            ((1,), (1,)),
        )
        growth = jnp.exp(mode_row(columns) * step)
        cells = jnp.sum(own_group(weighted, SUB) * growth, axis=0, keepdims=True)
        for a in range(2):
            base = (a * all_tiles + tile) * 17
            sent_ref[base : base + 8, :] = summary[a * half : (a + 1) * half]
            sent_ref[base + 8 : base + 16, :] = tail[a * half : (a + 1) * half]
            sent_ref[base + 16 : base + 17, :] = cells

    def arrived(q):
        loads[1 + 2 * q].wait()
        loads[2 + 2 * q].wait()

    def of_step(q):
        return range(q * tiles, (q + 1) * tiles)

    arrived(0)
    for tile in of_step(0):
        pair_tile(tile)
    loads[0].wait()
    rates = rates_ref[...]
    stores = []
    for q in range(HALVES):
        if q + 1 < HALVES:
            arrived(q + 1)
            for tile in of_step(q + 1):
                pair_tile(tile)
        for tile in of_step(q):
            one_tile(tile, rates)
        for a in range(2):
            at = pl.ds((a * HALVES + q) * chunk, chunk)
            stores.append(
                pltpu.make_async_copy(
                    sent_ref.at[at], out_hbm.at[at], sent_sems.at[a * HALVES + q]
                )
            )
            stores[-1].start()
    for store in stores:
        store.wait()


def local_kernel(rates_ref, rate_row_ref, amp_row_ref, grad_ref, out_ref, near_ref, far_ref):
    rows = grad_ref.shape[0]
    modes = rates_ref.shape[0]
    tiles = grad_ref.shape[1] // LANES
    pos = iota((modes, LANES), 1).astype(F32)
    step = iota((SUB, LANES), 0).astype(F32)
    later = iota((GT, SUB, LANES), 2) >= iota((GT, SUB, LANES), 1)
    later = later.reshape(GT * SUB, LANES)
    blocks = rows // SUB
    to_next = (SUB - iota((SUB, LANES), 0)).astype(F32)
    to_end = (SUB * (blocks - 1 - iota((blocks, LANES), 0))).astype(F32)

    def one_tile(k, carry):
        tile = pl.program_id(0) * tiles + k
        at = pl.ds(pl.multiple_of(k * LANES, LANES), LANES)
        grad = grad_ref[:, at]
        columns = group_columns(rates_ref[...], tile * GT)
        high, low = split(jnp.concatenate([jnp.exp(-r * pos) for r in columns], 0))
        amp_row = amp_row_ref[:, at]
        rate_row = rate_row_ref[:, at]
        grown = [on_diagonal(part) for part in split(amp_row * jnp.exp(rate_row * step))]
        kernel = dot(
            jnp.concatenate([grown[0], grown[1], grown[0]], 1),
            jnp.concatenate([high, high, low], 0),
        )
        left = jnp.concatenate(split(jnp.where(later, kernel, 0.0)), 1)
        wide = windows(grad)
        full = dot(left, jnp.concatenate([wide, wide], 0))
        for i in range(rows // SUB):
            out_ref[i * SUB : (i + 1) * SUB, at] = own_group(
                full[:, i * LANES : (i + 1) * LANES], SUB
            )
        near_ref[:, at] = amp_row * jnp.exp(-rate_row * to_next)
        far_ref[:, at] = jnp.exp(-rate_row * to_end)
        return carry

    lax.fori_loop(0, tiles, one_tile, 0, unroll=8)


def scan_kernel(half_ref, decay_ref, in_ref, out_ref):
    shards = in_ref.shape[0] // 17
    decay = decay_ref[...]
    state = jnp.zeros((8, LANES), F32)
    total = jnp.zeros((8, LANES), F32)
    row = jnp.zeros((1, LANES), F32)
    for j in reversed(range(shards)):
        out_ref[9 * j : 9 * j + 8, :] = state
        total = total + in_ref[17 * j + 8 : 17 * j + 16, :] * state
        row = row + in_ref[17 * j + 16 : 17 * j + 17, :]
        state = in_ref[17 * j : 17 * j + 8, :] + decay * state
    same = iota((2 * LANES, LANES), 0) // CG % GT == iota((2 * LANES, LANES), 1) // CG
    summed = dot(jnp.concatenate(split(total), 1), same.astype(F32).astype(BF16))
    place = iota((8, LANES), 1) % CG == iota((8, LANES), 0) + half_ref[0]
    row = row + jnp.sum(jnp.where(place, summed, 0.0), axis=0, keepdims=True)
    own = iota((1, LANES), 1) % CG - half_ref[0]
    row = jnp.where((own >= 0) & (own < 8), row, 0.0)
    for j in range(shards):
        out_ref[9 * j + 8 : 9 * j + 9, :] = row


def carry_kernel(state_ref, local_ref, near_ref, far_ref, out_hbm, out_ref, sems):
    rows, width = out_ref.shape
    all_tiles = width // LANES
    block = width // PIECES
    stores = []
    for tile in range(all_tiles):
        at = pl.ds(tile * LANES, LANES)
        state = jnp.concatenate(
            [state_ref[pl.ds((a * all_tiles + tile) * 9, 8), :] for a in range(2)], 0
        )
        rights = [on_diagonal(part) for part in split(state)]
        near = near_ref[:, at]
        far = far_ref[:, at]
        high, low = split(
            jnp.concatenate([near * far[i : i + 1] for i in range(rows // SUB)], 0)
        )
        left = jnp.concatenate([high, low, high], 1)
        right = jnp.concatenate([rights[0], rights[0], rights[1]], 0)
        out_ref[:, at] = local_ref[:, at] + dot(left, right)
        if (tile + 1) % (all_tiles // PIECES) == 0:
            q = tile // (all_tiles // PIECES)
            at = pl.ds(q * block, block)
            stores.append(
                pltpu.make_async_copy(out_ref.at[:, at], out_hbm.at[:, at], sems.at[q])
            )
            stores[-1].start()
    for store in stores:
        store.wait()


def finish_kernel(factor_ref, a_ref, b_ref, c_ref, d_ref, out_ref):
    total = (a_ref[...] + b_ref[...]) + (c_ref[...] + d_ref[...])
    count = total.shape[0]
    groups = out_ref.shape[1]
    pick = iota((2 * count, groups), 0) % count == iota((2 * count, groups), 1) // GT
    keep = iota((GT, CG, groups), 0) == iota((GT, CG, groups), 2) % GT
    spread = dot(
        jnp.concatenate(split(total), 0), pick.astype(F32).astype(BF16), ((0,), (0,))
    ).reshape(GT, CG, groups)
    out_ref[...] = jnp.sum(jnp.where(keep, spread, 0.0), axis=0) * factor_ref[...]


def whole(shape):
    return pl.BlockSpec(shape, lambda *_: (0,) * len(shape))


def local(grad_out, inputs, residues, rates):
    _, rows, width = grad_out.shape
    modes, groups = residues.shape
    tiles = width // LANES
    shards = lax.axis_size(CTX)
    seqs = lax.axis_size("seq_x") * lax.axis_size("seq_core")
    block = width // STEPS
    slab = pl.BlockSpec((rows, block), lambda q: (0, q))
    anywhere = pl.BlockSpec(memory_space=pl.ANY)
    grad = grad_out[0]
    inp = inputs[0]
    full = pltpu.CompilerParams(vmem_limit_bytes=60 * 1024 * 1024)
    vmem = pltpu.CompilerParams(vmem_limit_bytes=16 * 1024 * 1024)
    small = pltpu.CompilerParams(vmem_limit_bytes=8 * 1024 * 1024)

    sent = pl.pallas_call(
        summary_kernel,
        in_specs=[anywhere, anywhere, anywhere],
        out_specs=anywhere,
        out_shape=jax.ShapeDtypeStruct((shards * 17, LANES), F32),
        scratch_shapes=[
            pltpu.VMEM((modes, groups), F32),
            pltpu.VMEM((rows, width), BF16),
            pltpu.VMEM((rows, width), BF16),
            pltpu.VMEM((shards * 17, LANES), F32),
            pltpu.VMEM((tiles, LANES, 2 * LANES), BF16),
            pltpu.SemaphoreType.DMA((1 + 2 * HALVES,)),
            pltpu.SemaphoreType.DMA((2 * HALVES,)),
        ],
        compiler_params=full,
        name="summary",
    )(rates, grad, inp)
    got = lax.all_to_all(sent.reshape(shards, 1, 17 * LANES), CTX, 0, 0, tiled=True)

    amplitude = residues * jnp.sqrt(-jnp.expm1(-2.0 * rates) / modes)
    factor = jnp.sqrt(-jnp.expm1(-2.0 * rates) / float(seqs * shards * rows * (width // groups)))
    place = lax.axis_index(CTX)
    half = modes // 2
    first_mode = place // tiles * half
    own_rates = lax.dynamic_slice(rates, (first_mode, place % tiles * GT), (half, GT))
    decay = jnp.repeat(jnp.exp(-own_rates * rows), CG, axis=1)

    row = pl.BlockSpec((1, block), lambda q: (0, q))
    local_in, near, far = pl.pallas_call(
        local_kernel,
        grid=(STEPS,),
        in_specs=[whole((modes, groups)), row, row, slab],
        out_specs=[
            slab,
            pl.BlockSpec((SUB, block), lambda q: (0, q)),
            pl.BlockSpec((rows // SUB, block), lambda q: (0, q)),
        ],
        out_shape=[
            jax.ShapeDtypeStruct((rows, width), F32),
            jax.ShapeDtypeStruct((SUB, width), F32),
            jax.ShapeDtypeStruct((rows // SUB, width), F32),
        ],
        compiler_params=vmem,
        name="local",
        cost_estimate=pl.CostEstimate(
            flops=8 * 10**9, bytes_accessed=5 * 2**20, transcendentals=10**6
        ),
    )(rates, rates.T.reshape(1, width), amplitude.T.reshape(1, width), grad)

    got, local_in = lax.optimization_barrier((got, local_in))
    states = pl.pallas_call(
        scan_kernel,
        in_specs=[
            pl.BlockSpec(memory_space=pltpu.SMEM),
            whole((half, LANES)),
            whole((shards * 17, LANES)),
        ],
        out_shape=jax.ShapeDtypeStruct((shards * 9, LANES), F32),
        compiler_params=small,
        name="scan",
    )(first_mode[None], decay, got.reshape(shards * 17, LANES))
    back = lax.all_to_all(states.reshape(shards, 1, 9 * LANES), CTX, 0, 0, tiled=True)

    sums = back[:, 0, 8 * LANES :]
    mine = sums[:tiles] + sums[tiles:]
    others = [mine]
    for bits in (1, 2, 3):
        pairs = [(d, d ^ bits) for d in range(4)]
        others.append(lax.ppermute(mine, ("seq_x", "seq_core"), pairs))
    grad_in = pl.pallas_call(
        carry_kernel,
        in_specs=[
            whole((shards * 9, LANES)),
            whole((rows, width)),
            whole((SUB, width)),
            whole((rows // SUB, width)),
        ],
        out_specs=anywhere,
        out_shape=jax.ShapeDtypeStruct((rows, width), F32),
        scratch_shapes=[pltpu.VMEM((rows, width), F32), pltpu.SemaphoreType.DMA((PIECES,))],
        compiler_params=vmem,
        name="carry",
        cost_estimate=pl.CostEstimate(
            flops=8 * 10**8, bytes_accessed=7 * 2**20, transcendentals=0
        ),
    )(back.reshape(shards * 9, LANES), local_in, near, far)
    grad_res = pl.pallas_call(
        finish_kernel,
        out_shape=jax.ShapeDtypeStruct((modes, groups), F32),
        compiler_params=small,
        name="finish",
    )(factor, *others)
    return grad_in[None], grad_res


def solution(mesh):
    torus = Mesh(
        mesh.devices.reshape(2, 2, 2, 8, 4), ("seq_x", "seq_core", "ctx_0", "ctx_1", "ctx_2")
    )
    seq = ("seq_x", "seq_core")
    return jax.shard_map(
        local,
        mesh=torus,
        in_specs=(P(seq, CTX, None), P(seq, CTX, None), P(), P()),
        out_specs=(P(seq, CTX, None), P()),
        check_vma=False,
    )
```

```python
import jax
import jax.numpy as jnp
from jax import lax
from jax.experimental import pallas as pl
from jax.experimental.pallas import tpu as pltpu
from jax.sharding import Mesh
from jax.sharding import PartitionSpec as P

CTX = ("ctx_0", "ctx_1", "ctx_2")
LANES = 128
CG = 16
GT = LANES // CG
SUB = 16
STEPS = 4
HALVES = 2
PIECES = 16
F32 = jnp.float32
BF16 = jnp.bfloat16


def iota(shape, dim):
    return lax.broadcasted_iota(jnp.int32, shape, dim)


def split(value):
    high = value.astype(BF16)
    return high, (value - high.astype(F32)).astype(BF16)


def dot(a, b, dims=((1,), (0,))):
    return lax.dot_general(a, b, (dims, ((), ())), preferred_element_type=F32)


def group_columns(table, first):
    groups = table.shape[1]
    turned = pltpu.roll(table, (groups - first) % groups, 1)
    return [jnp.broadcast_to(turned[:, g : g + 1], (table.shape[0], LANES)) for g in range(GT)]


def own_group(full, rows):
    group_of = iota((rows, LANES), 1) // CG
    kept = full[:rows]
    for g in range(1, GT):
        kept = jnp.where(group_of == g, full[g * rows : (g + 1) * rows], kept)
    return kept


def on_diagonal(part):
    group_of = iota(part.shape, 1) // CG
    zero = jnp.zeros_like(part)
    return jnp.concatenate([jnp.where(group_of == g, part, zero) for g in range(GT)], 0)


def windows(piece):
    shifted = [piece]
    for first in range(SUB, piece.shape[0], SUB):
        shifted.append(jnp.concatenate([piece[first:], jnp.zeros((first, LANES), BF16)], 0))
    return jnp.concatenate(shifted, 1)


def mode_row(columns):
    modes = columns[0].shape[0]
    ahead = iota((modes, LANES), 1) - iota((modes, LANES), 0)
    placed = jnp.where(ahead == 0, columns[0], 0.0)
    for g in range(1, GT):
        placed = jnp.where(ahead == g * CG, columns[g], placed)
    return jnp.sum(placed, axis=0, keepdims=True)


def summary_kernel(
    rates_hbm, grad_hbm, in_hbm, out_hbm, rates_ref, grad_ref, in_ref, sent_ref, pair_ref, sems, sent_sems
):
    rows, width = grad_ref.shape
    modes = rates_ref.shape[0]
    half = modes // 2
    all_tiles = width // LANES
    tiles = all_tiles // HALVES
    block = tiles * LANES
    chunk = tiles * 17
    loads = [pltpu.make_async_copy(rates_hbm, rates_ref, sems.at[0])]
    for q in range(HALVES):
        at = pl.ds(q * block, block)
        for i, (source, into) in enumerate(((grad_hbm, grad_ref), (in_hbm, in_ref))):
            loads.append(
                pltpu.make_async_copy(source.at[:, at], into.at[:, at], sems.at[1 + 2 * q + i])
            )
    for load in loads:
        load.start()
    pos = iota((modes, LANES), 1).astype(F32)
    step = iota((SUB, LANES), 0).astype(F32)
    later = iota((GT, SUB, LANES), 2) >= iota((GT, SUB, LANES), 1)
    later = later.reshape(GT * SUB, LANES)

    def pair_tile(tile):
        at = pl.ds(tile * LANES, LANES)
        inp = in_ref[:, at]
        left = jnp.concatenate(
            [on_diagonal(inp[i : i + SUB]) for i in range(0, rows, SUB)], 1
        )
        pairs = dot(left, windows(grad_ref[:, at]), ((1,), (1,)))
        high, low = split(jnp.where(later, pairs, 0.0))
        pair_ref[tile, :, :LANES] = high
        pair_ref[tile, :, LANES:] = low

    def one_tile(tile, rates):
        at = pl.ds(tile * LANES, LANES)
        grad = grad_ref[:, at]
        inp = in_ref[:, at]
        columns = group_columns(rates, tile * GT)
        high, low = split(jnp.concatenate([jnp.exp(-r * pos) for r in columns], 0))
        left = jnp.concatenate([high, low], 1)
        summary = own_group(dot(left, jnp.concatenate([grad, grad], 0)), modes)
        tails = jnp.concatenate([jnp.exp(-r * (rows - pos)) for r in columns], 0)
        left = jnp.concatenate(split(tails), 1)
        tail = own_group(dot(left, jnp.concatenate([inp, inp], 0)), modes)
        pairs = pair_ref[tile]
        weighted = dot(
            jnp.concatenate([pairs, pairs[:, :LANES]], 1),
            jnp.concatenate([high, high, low], 1),
            ((1,), (1,)),
        )
        growth = jnp.exp(mode_row(columns) * step)
        cells = jnp.sum(own_group(weighted, SUB) * growth, axis=0, keepdims=True)
        for a in range(2):
            base = (a * all_tiles + tile) * 17
            sent_ref[base : base + 8, :] = summary[a * half : (a + 1) * half]
            sent_ref[base + 8 : base + 16, :] = tail[a * half : (a + 1) * half]
            sent_ref[base + 16 : base + 17, :] = cells

    def arrived(q):
        loads[1 + 2 * q].wait()
        loads[2 + 2 * q].wait()

    def of_step(q):
        return range(q * tiles, (q + 1) * tiles)

    arrived(0)
    for tile in of_step(0):
        pair_tile(tile)
    loads[0].wait()
    rates = rates_ref[...]
    stores = []
    for q in range(HALVES):
        if q + 1 < HALVES:
            arrived(q + 1)
            for tile in of_step(q + 1):
                pair_tile(tile)
        for tile in of_step(q):
            one_tile(tile, rates)
        for a in range(2):
            at = pl.ds((a * HALVES + q) * chunk, chunk)
            stores.append(
                pltpu.make_async_copy(
                    sent_ref.at[at], out_hbm.at[at], sent_sems.at[a * HALVES + q]
                )
            )
            stores[-1].start()
    for store in stores:
        store.wait()


def local_kernel(rates_ref, rate_row_ref, amp_row_ref, grad_ref, out_ref, near_ref, far_ref):
    rows = grad_ref.shape[0]
    modes = rates_ref.shape[0]
    tiles = grad_ref.shape[1] // LANES
    pos = iota((modes, LANES), 1).astype(F32)
    step = iota((SUB, LANES), 0).astype(F32)
    later = iota((GT, SUB, LANES), 2) >= iota((GT, SUB, LANES), 1)
    later = later.reshape(GT * SUB, LANES)
    blocks = rows // SUB
    to_next = (SUB - iota((SUB, LANES), 0)).astype(F32)
    to_end = (SUB * (blocks - 1 - iota((blocks, LANES), 0))).astype(F32)

    def one_tile(k, carry):
        tile = pl.program_id(0) * tiles + k
        at = pl.ds(pl.multiple_of(k * LANES, LANES), LANES)
        grad = grad_ref[:, at]
        columns = group_columns(rates_ref[...], tile * GT)
        high, low = split(jnp.concatenate([jnp.exp(-r * pos) for r in columns], 0))
        amp_row = amp_row_ref[:, at]
        rate_row = rate_row_ref[:, at]
        grown = [on_diagonal(part) for part in split(amp_row * jnp.exp(rate_row * step))]
        kernel = dot(
            jnp.concatenate([grown[0], grown[1], grown[0]], 1),
            jnp.concatenate([high, high, low], 0),
        )
        left = jnp.concatenate(split(jnp.where(later, kernel, 0.0)), 1)
        wide = windows(grad)
        full = dot(left, jnp.concatenate([wide, wide], 0))
        for i in range(rows // SUB):
            out_ref[i * SUB : (i + 1) * SUB, at] = own_group(
                full[:, i * LANES : (i + 1) * LANES], SUB
            )
        near_ref[:, at] = amp_row * jnp.exp(-rate_row * to_next)
        far_ref[:, at] = jnp.exp(-rate_row * to_end)
        return carry

    lax.fori_loop(0, tiles, one_tile, 0, unroll=8)


def scan_kernel(half_ref, decay_ref, in_ref, out_ref):
    shards = in_ref.shape[0] // 17
    decay = decay_ref[...]
    state = jnp.zeros((8, LANES), F32)
    total = jnp.zeros((8, LANES), F32)
    row = jnp.zeros((1, LANES), F32)
    for j in reversed(range(shards)):
        out_ref[9 * j : 9 * j + 8, :] = state
        total = total + in_ref[17 * j + 8 : 17 * j + 16, :] * state
        row = row + in_ref[17 * j + 16 : 17 * j + 17, :]
        state = in_ref[17 * j : 17 * j + 8, :] + decay * state
    same = iota((2 * LANES, LANES), 0) // CG % GT == iota((2 * LANES, LANES), 1) // CG
    summed = dot(jnp.concatenate(split(total), 1), same.astype(F32).astype(BF16))
    place = iota((8, LANES), 1) % CG == iota((8, LANES), 0) + half_ref[0]
    row = row + jnp.sum(jnp.where(place, summed, 0.0), axis=0, keepdims=True)
    own = iota((1, LANES), 1) % CG - half_ref[0]
    row = jnp.where((own >= 0) & (own < 8), row, 0.0)
    for j in range(shards):
        out_ref[9 * j + 8 : 9 * j + 9, :] = row


def carry_kernel(state_ref, local_ref, near_ref, far_ref, out_hbm, out_ref, sems):
    rows, width = out_ref.shape
    all_tiles = width // LANES
    block = width // PIECES
    stores = []
    for tile in range(all_tiles):
        at = pl.ds(tile * LANES, LANES)
        state = jnp.concatenate(
            [state_ref[pl.ds((a * all_tiles + tile) * 9, 8), :] for a in range(2)], 0
        )
        rights = [on_diagonal(part) for part in split(state)]
        near = near_ref[:, at]
        far = far_ref[:, at]
        high, low = split(
            jnp.concatenate([near * far[i : i + 1] for i in range(rows // SUB)], 0)
        )
        left = jnp.concatenate([high, low, high], 1)
        right = jnp.concatenate([rights[0], rights[0], rights[1]], 0)
        out_ref[:, at] = local_ref[:, at] + dot(left, right)
        if (tile + 1) % (all_tiles // PIECES) == 0:
            q = tile // (all_tiles // PIECES)
            at = pl.ds(q * block, block)
            stores.append(
                pltpu.make_async_copy(out_ref.at[:, at], out_hbm.at[:, at], sems.at[q])
            )
            stores[-1].start()
    for store in stores:
        store.wait()


def finish_kernel(factor_ref, a_ref, b_ref, c_ref, d_ref, out_ref):
    total = (a_ref[...] + b_ref[...]) + (c_ref[...] + d_ref[...])
    count = total.shape[0]
    groups = out_ref.shape[1]
    pick = iota((2 * count, groups), 0) % count == iota((2 * count, groups), 1) // GT
    keep = iota((GT, CG, groups), 0) == iota((GT, CG, groups), 2) % GT
    spread = dot(
        jnp.concatenate(split(total), 0), pick.astype(F32).astype(BF16), ((0,), (0,))
    ).reshape(GT, CG, groups)
    out_ref[...] = jnp.sum(jnp.where(keep, spread, 0.0), axis=0) * factor_ref[...]


def whole(shape):
    return pl.BlockSpec(shape, lambda *_: (0,) * len(shape))


def local(grad_out, inputs, residues, rates):
    _, rows, width = grad_out.shape
    modes, groups = residues.shape
    tiles = width // LANES
    shards = lax.axis_size(CTX)
    seqs = lax.axis_size("seq_x") * lax.axis_size("seq_core")
    block = width // STEPS
    slab = pl.BlockSpec((rows, block), lambda q: (0, q))
    anywhere = pl.BlockSpec(memory_space=pl.ANY)
    grad = grad_out[0]
    inp = inputs[0]
    full = pltpu.CompilerParams(vmem_limit_bytes=60 * 1024 * 1024)
    vmem = pltpu.CompilerParams(vmem_limit_bytes=16 * 1024 * 1024)
    small = pltpu.CompilerParams(vmem_limit_bytes=8 * 1024 * 1024)

    sent = pl.pallas_call(
        summary_kernel,
        in_specs=[anywhere, anywhere, anywhere],
        out_specs=anywhere,
        out_shape=jax.ShapeDtypeStruct((shards * 17, LANES), F32),
        scratch_shapes=[
            pltpu.VMEM((modes, groups), F32),
            pltpu.VMEM((rows, width), BF16),
            pltpu.VMEM((rows, width), BF16),
            pltpu.VMEM((shards * 17, LANES), F32),
            pltpu.VMEM((tiles, LANES, 2 * LANES), BF16),
            pltpu.SemaphoreType.DMA((1 + 2 * HALVES,)),
            pltpu.SemaphoreType.DMA((2 * HALVES,)),
        ],
        compiler_params=full,
        name="summary",
    )(rates, grad, inp)
    got = lax.all_to_all(sent.reshape(shards, 1, 17 * LANES), CTX, 0, 0, tiled=True)

    amplitude = residues * jnp.sqrt(-jnp.expm1(-2.0 * rates) / modes)
    factor = jnp.sqrt(-jnp.expm1(-2.0 * rates) / float(seqs * shards * rows * (width // groups)))
    place = lax.axis_index(CTX)
    half = modes // 2
    first_mode = place // tiles * half
    own_rates = lax.dynamic_slice(rates, (first_mode, place % tiles * GT), (half, GT))
    decay = jnp.repeat(jnp.exp(-own_rates * rows), CG, axis=1)

    row = pl.BlockSpec((1, block), lambda q: (0, q))
    local_in, near, far = pl.pallas_call(
        local_kernel,
        grid=(STEPS,),
        in_specs=[whole((modes, groups)), row, row, slab],
        out_specs=[
            slab,
            pl.BlockSpec((SUB, block), lambda q: (0, q)),
            pl.BlockSpec((rows // SUB, block), lambda q: (0, q)),
        ],
        out_shape=[
            jax.ShapeDtypeStruct((rows, width), F32),
            jax.ShapeDtypeStruct((SUB, width), F32),
            jax.ShapeDtypeStruct((rows // SUB, width), F32),
        ],
        compiler_params=vmem,
        name="local",
        cost_estimate=pl.CostEstimate(
            flops=8 * 10**9, bytes_accessed=5 * 2**20, transcendentals=10**6
        ),
    )(rates, rates.T.reshape(1, width), amplitude.T.reshape(1, width), grad)

    got, local_in = lax.optimization_barrier((got, local_in))
    states = pl.pallas_call(
        scan_kernel,
        in_specs=[
            pl.BlockSpec(memory_space=pltpu.SMEM),
            whole((half, LANES)),
            whole((shards * 17, LANES)),
        ],
        out_shape=jax.ShapeDtypeStruct((shards * 9, LANES), F32),
        compiler_params=small,
        name="scan",
    )(first_mode[None], decay, got.reshape(shards * 17, LANES))
    back = lax.all_to_all(states.reshape(shards, 1, 9 * LANES), CTX, 0, 0, tiled=True)

    sums = back[:, 0, 8 * LANES :]
    mine = sums[:tiles] + sums[tiles:]
    others = [mine]
    for bits in (1, 2, 3):
        pairs = [(d, d ^ bits) for d in range(4)]
        others.append(lax.ppermute(mine, ("seq_x", "seq_core"), pairs))
    grad_in = pl.pallas_call(
        carry_kernel,
        in_specs=[
            whole((shards * 9, LANES)),
            whole((rows, width)),
            whole((SUB, width)),
            whole((rows // SUB, width)),
        ],
        out_specs=anywhere,
        out_shape=jax.ShapeDtypeStruct((rows, width), F32),
        scratch_shapes=[pltpu.VMEM((rows, width), F32), pltpu.SemaphoreType.DMA((PIECES,))],
        compiler_params=vmem,
        name="carry",
        cost_estimate=pl.CostEstimate(
            flops=8 * 10**8, bytes_accessed=7 * 2**20, transcendentals=0
        ),
    )(back.reshape(shards * 9, LANES), local_in, near, far)
    grad_res = pl.pallas_call(
        finish_kernel,
        out_shape=jax.ShapeDtypeStruct((modes, groups), F32),
        compiler_params=small,
        name="finish",
    )(factor, *others)
    return grad_in[None], grad_res


def solution(mesh):
    torus = Mesh(
        mesh.devices.reshape(2, 2, 2, 8, 4), ("seq_x", "seq_core", "ctx_0", "ctx_1", "ctx_2")
    )
    seq = ("seq_x", "seq_core")
    return jax.shard_map(
        local,
        mesh=torus,
        in_specs=(P(seq, CTX, None), P(seq, CTX, None), P(), P()),
        out_specs=(P(seq, CTX, None), P()),
        check_vma=False,
    )
```
